32 devices in a mesh: row: 16 (over z, y, x), col: 2 (over core).
Axes of the slice: x: 2, y: 2, z: 4, core: 2. Of those that a mesh axis runs over, the one named last changes fastest.
Arguments:
- panel: bfloat16 [65536, 256], P('row'), may hold values from -400 to 400, as said below
- slab: bfloat16 [65536, 1024], P('row', 'col'), may hold values from -300 to 300
Outputs:
- factor: float32 [256, 256], P(None, 'col')
- coupling: float32 [256, 1024], P(None, 'col')
- remainder: bfloat16 [65536, 1024], P('row', 'col')
The draws below stay inside these ranges and needn't reach their ends.
Inputs may be any that keep to these rules, and one draw needn't show every extreme that they name: panel has full column rank.
All inputs are finite; a program needn't handle non-finite values.
Results may differ from the reference program's by a relative error of at most 0.015.
The reference program's roundings to bfloat16 on the way (of `update`) count: a program that leaves them out, or rounds other values in their place, can miss the bound.
Values sent between devices are 32-bit elements; how exact they have to be, the bound alone decides.
A program may use at most 64 MiB of HBM per device.

```python
import jax
import jax.numpy as jnp
from jax import lax

K = 256
SLAB = 1024
M = 65536


def panel_values(key):
    base = jax.random.fold_in(key, 7)
    keys = jax.random.split(base, 3)
    raw = jax.random.normal(keys[0], (M, K), jnp.float32)
    mixing = jnp.eye(K, dtype=jnp.float32) + 0.5 * jax.random.normal(keys[1], (K, K), jnp.float32) / jnp.sqrt(K * 1.0)
    column_scale = jnp.exp(jax.random.uniform(keys[2], (K,), jnp.float32, jnp.log(0.5), jnp.log(2.0)))
    trend = 1.0 + 2.0 * jnp.arange(M, dtype=jnp.float32) / M
    row_scale = trend
    values = jnp.dot(raw, mixing) * column_scale[None, :] * row_scale[:, None]
    return jnp.clip(values, -400.0, 400.0)


def draw_panel(key, part):
    return panel_values(key).astype(jnp.bfloat16)


def draw_slab(key, part):
    values = panel_values(key)
    keys = jax.random.split(jax.random.fold_in(key, 13), 2)
    mixing = jax.random.normal(keys[0], (K, SLAB), jnp.float32) / jnp.sqrt(K * 1.0)
    noise = 0.5 * jax.random.normal(keys[1], (M, SLAB), jnp.float32)
    return jnp.clip(jnp.dot(values, mixing) + noise, -300.0, 300.0).astype(jnp.bfloat16)


def setup_inputs(seed: int = 0) -> dict:
    streams_of = jax.random.split(jax.random.key(seed), 3)
    return {
        "panel": draw_panel(jax.random.fold_in(streams_of[2], 71), 0),
        "slab": draw_slab(jax.random.fold_in(streams_of[2], 71), 0),
    }


def reference(panel, slab):
    total_rows = panel.shape[0]
    wide_panel = panel.astype(jnp.float32)
    wide_slab = slab.astype(jnp.float32)
    gram = jnp.dot(wide_panel.T, wide_panel, precision=lax.Precision.HIGHEST) / total_rows
    factor = jnp.linalg.cholesky(gram).T
    cross = jnp.dot(wide_panel.T, wide_slab, precision=lax.Precision.HIGHEST) / total_rows
    coupling = lax.linalg.triangular_solve(factor, cross, left_side=True, lower=False, transpose_a=True)
    update = lax.linalg.triangular_solve(factor, coupling, left_side=True, lower=False, transpose_a=False)
    update = update.astype(jnp.bfloat16)
    remainder = (wide_slab - jnp.dot(panel.astype(jnp.float32), update.astype(jnp.float32), preferred_element_type=jnp.float32)).astype(jnp.bfloat16)
    return (factor, coupling, remainder)
```

```python
import functools

import jax
import jax.numpy as jnp
from jax import lax
from jax.experimental import pallas as pl
from jax.experimental.pallas import tpu as pltpu

HI = lax.Precision.HIGHEST
MESH = pl.DeviceIdType.MESH


def mm(a, b, ca=1, cb=0):
    return lax.dot_general(a, b, (((ca,), (cb,)), ((), ())), precision=HI, preferred_element_type=jnp.float32)


def eliminate(block, r_ref, w_ref):
    n = block.shape[0]
    groups = n // 8
    lane = lax.broadcasted_iota(jnp.int32, (8, n), 1)
    sub = lax.broadcasted_iota(jnp.int32, (8, n), 0)
    a = [block[8 * t : 8 * t + 8, :] for t in range(groups)]
    w = [jnp.where(lane == sub + 8 * t, 1.0, 0.0).astype(jnp.float32) for t in range(groups)]

    def group(g, carry):
        a, w = list(carry[0]), list(carry[1])
        for j in range(8):
            inv = lax.rsqrt(jnp.broadcast_to(a[0][j : j + 1, j : j + 1], (8, n)))
            arow = jnp.broadcast_to(a[0][j : j + 1, :], (8, n)) * inv
            wrow = jnp.broadcast_to(w[0][j : j + 1, :], (8, n)) * inv
            for t in range(groups):
                col = jnp.broadcast_to(a[t][:, j : j + 1], (8, n)) * inv
                if t == 0:
                    below = sub > j
                    here = sub == j
                    a[0], w[0] = (
                        jnp.where(here, arow, jnp.where(below, a[0] - col * arow, a[0])),
                        jnp.where(here, wrow, jnp.where(below, w[0] - col * wrow, w[0])),
                    )
                else:
                    a[t] = a[t] - col * arow
                    w[t] = w[t] - col * wrow
        start = pl.multiple_of(8 * g, 8)
        r = pltpu.roll(a[0], 8 * g, 1)
        r_ref[pl.ds(start, 8), :] = jnp.where(lane >= sub + 8 * g, r, 0.0)
        w_ref[pl.ds(start, 8), :] = w[0]
        zero = jnp.zeros((8, n), jnp.float32)
        a = [pltpu.roll(x, n - 8, 1) for x in a[1:]] + [zero]
        w = w[1:] + [zero]
        return tuple(a), tuple(w)

    lax.fori_loop(0, groups, group, (tuple(a), tuple(w)))


def factor_kernel(gram_ref, factor_ref, invt_ref, r_ref, w_ref):
    h = gram_ref.shape[1]
    eliminate(gram_ref[:h, :], r_ref, w_ref)
    w1 = w_ref[...]
    factor_ref[:h, :h] = r_ref[...]
    invt_ref[:h, :h] = w1
    r12 = mm(w1, gram_ref[h : 2 * h, :])
    factor_ref[:h, h:] = r12
    factor_ref[h:, :h] = jnp.zeros((h, h), jnp.float32)
    invt_ref[:h, h:] = jnp.zeros((h, h), jnp.float32)
    eliminate(gram_ref[2 * h :, :] - mm(r12, r12, 0, 0), r_ref, w_ref)
    w2 = w_ref[...]
    factor_ref[h:, h:] = r_ref[...]
    invt_ref[h:, h:] = w2
    invt_ref[h:, :h] = -mm(w2, mm(r12, w1, 0, 0))


def factor_and_invt(blocks):
    h = blocks.shape[1]
    n = 2 * h
    out = jax.ShapeDtypeStruct((n, n), jnp.float32)
    return pl.pallas_call(
        factor_kernel,
        out_shape=(out, out),
        scratch_shapes=[pltpu.VMEM((h, h), jnp.float32), pltpu.VMEM((h, h), jnp.float32)],
        cost_estimate=pl.CostEstimate(flops=60_000_000, bytes_accessed=3 * n * n * 4, transcendentals=n),
        name="factor",
    )(blocks)


def levels(rows):
    inner = 1
    while inner * inner * 4 <= rows:
        inner *= 2
    return inner, rows // inner


def sums_kernel(
    inner, outer, cols, split, scale,
    panel_hbm, slab_hbm, gram_out, cross_out,
    panel, slab, g_own, g_in, g_mid, g_all, x_own, x_in, x_mid, x_mid_in, x_all,
    load_sem, g_sem, x_sem, out_sem,
):
    row = lax.axis_index("row")
    col = lax.axis_index("col")
    high, low = row // inner, row % inner
    f32 = jnp.float32

    def near(d):
        return high * inner + (low + d) % inner

    def far(d):
        return ((high + d) % outer) * inner + low

    chunks = panel.shape[0] // load_sem.shape[1]
    steps = load_sem.shape[1]
    loads = []
    for t in range(steps):
        part = pl.ds(t * chunks, chunks)
        loads.append(pltpu.make_async_copy(panel_hbm.at[part], panel.at[part], load_sem.at[0, t]))
    for t in range(steps):
        part = pl.ds(t * chunks, chunks)
        loads.append(pltpu.make_async_copy(slab_hbm.at[part], slab.at[part], load_sem.at[1, t]))
    for copy in loads:
        copy.start()

    barrier = pltpu.get_barrier_semaphore()
    greeted = 0
    for d in range(inner):
        for e in range(cols if split > 1 else 1):
            if d or e:
                pl.semaphore_signal(barrier, 1, device_id={"row": near(d), "col": (col + e) % cols}, device_id_type=MESH)
                greeted += 1
    for d in range(1, outer):
        pl.semaphore_signal(barrier, 1, device_id={"row": far(d), "col": col}, device_id_type=MESH)
        greeted += 1

    def send(src, dst, sems, index, to_row, to_col):
        copy = pltpu.make_async_remote_copy(
            src_ref=src, dst_ref=dst, send_sem=sems.at[0, index], recv_sem=sems.at[1, index],
            device_id={"row": to_row, "col": to_col}, device_id_type=MESH,
        )
        copy.start()
        return copy

    def tdot(a, b):
        return lax.dot_general(a, b, (((0,), (0,)), ((), ())), preferred_element_type=f32)

    h = g_own.shape[1]
    acc = None
    for t in range(steps):
        loads[t].wait()
        p = panel[t * chunks : (t + 1) * chunks, :]
        term = tdot(p, p)
        acc = term if acc is None else acc + term
    acc = acc * scale
    g_own[:h, :] = acc[:h, :h]
    g_own[h : 2 * h, :] = acc[:h, h:]
    g_own[2 * h :, :] = acc[h:, h:]

    pl.semaphore_wait(barrier, greeted)

    share = g_own.shape[0] // split
    piece = share // inner
    base = (col * share) if split > 1 else 0
    g1 = []
    for d in range(1, inner):
        at = pl.multiple_of(base + ((low + d) % inner) * piece, 8)
        g1.append(send(g_own.at[pl.ds(at, piece)], g_in.at[d - 1], g_sem, d - 1, near(d), col))
    used = inner - 1

    acc = None
    for t in range(steps):
        loads[steps + t].wait()
        term = tdot(panel[t * chunks : (t + 1) * chunks, :], slab[t * chunks : (t + 1) * chunks, :])
        acc = term if acc is None else acc + term
    x_own[...] = acc * scale

    xp = x_own.shape[0] // inner
    x1 = []
    for d in range(1, inner):
        at = pl.multiple_of(((low + d) % inner) * xp, 8)
        x1.append(send(x_own.at[pl.ds(at, xp)], x_in.at[d - 1], x_sem, d - 1, near(d), col))
    xused = inner - 1

    mine = pl.multiple_of(base + low * piece, 8)
    total = g_own[pl.ds(mine, piece), :]
    for d in range(1, inner):
        g1[d - 1].wait()
        total = total + g_in[d - 1]
    g_mid[high] = total
    g2 = []
    for d in range(1, outer):
        g2.append(send(g_mid.at[high], g_mid.at[high], g_sem, used + d - 1, far(d), col))
    used += outer - 1
    for copy in g2:
        copy.wait()
    total = g_mid[0]
    for q in range(1, outer):
        total = total + g_mid[q]
    g_all[pl.ds(mine, piece), :] = total
    g3 = []
    for d in range(inner):
        for e in range(cols if split > 1 else 1):
            if d or e:
                part = g_all.at[pl.ds(mine, piece)]
                g3.append(send(part, part, g_sem, used, near(d), (col + e) % cols))
                used += 1

    at = pl.multiple_of(low * xp, 8)
    total = x_own[pl.ds(at, xp), :]
    for d in range(1, inner):
        x1[d - 1].wait()
        total = total + x_in[d - 1]
    xq = xp // outer
    if xq % 8 == 0:
        x_mid[...] = total
        x2 = []
        for d in range(1, outer):
            there = pl.multiple_of(((high + d) % outer) * xq, 8)
            x2.append(send(x_mid.at[pl.ds(there, xq)], x_mid_in.at[d - 1], x_sem, xused + d - 1, far(d), col))
        xused += outer - 1
        here = pl.multiple_of(high * xq, 8)
        total = x_mid[pl.ds(here, xq), :]
        for d in range(1, outer):
            x2[d - 1].wait()
            total = total + x_mid_in[d - 1]
        spot = pl.multiple_of(low * xp + high * xq, 8)
        x_all[pl.ds(spot, xq), :] = total
        x3 = []
        for d in range(1, outer):
            part = x_all.at[pl.ds(spot, xq)]
            x3.append(send(part, part, x_sem, xused + d - 1, far(d), col))
        xused += outer - 1
        for copy in x3:
            copy.wait()
    else:
        x_mid_in[high] = total
        x2 = []
        for d in range(1, outer):
            x2.append(send(x_mid_in.at[high], x_mid_in.at[high], x_sem, xused + d - 1, far(d), col))
        xused += outer - 1
        for copy in x2:
            copy.wait()
        total = x_mid_in[0]
        for q in range(1, outer):
            total = total + x_mid_in[q]
        x_all[pl.ds(at, xp), :] = total
    x4 = []
    for d in range(1, inner):
        part = x_all.at[pl.ds(at, xp)]
        x4.append(send(part, part, x_sem, xused + d - 1, near(d), col))

    for copy in g3:
        copy.wait()
    out = pltpu.make_async_copy(g_all, gram_out, out_sem.at[0])
    out.start()
    for copy in x4:
        copy.wait()
    out2 = pltpu.make_async_copy(x_all, cross_out, out_sem.at[1])
    out2.start()
    out.wait()
    out2.wait()


def sums(panel, slab, rows, cols):
    m, k = panel.shape
    width = slab.shape[1]
    inner, outer = levels(rows)
    h = k // 2
    split = cols if (3 * h) % (8 * inner * cols) == 0 else 1
    piece = 3 * h // split // inner
    xp = k // inner
    xq = xp // outer
    f32 = jnp.float32
    mid_in = (max(outer - 1, 1), xq, width) if xq % 8 == 0 else (outer, xp, width)
    g_copies = (inner - 1) + (outer - 1) + inner * (cols if split > 1 else 1) - 1
    x_copies = 2 * (inner - 1) + 2 * (outer - 1)
    steps = 4
    any_space = pl.BlockSpec(memory_space=pl.ANY)
    return pl.pallas_call(
        functools.partial(sums_kernel, inner, outer, cols, split, 1.0 / (m * rows)),
        out_shape=(jax.ShapeDtypeStruct((3 * h, h), f32), jax.ShapeDtypeStruct((k, width), f32)),
        in_specs=[any_space, any_space],
        out_specs=[any_space, any_space],
        scratch_shapes=[
            pltpu.VMEM((m, k), panel.dtype),
            pltpu.VMEM((m, width), slab.dtype),
            pltpu.VMEM((3 * h, h), f32),
            pltpu.VMEM((max(inner - 1, 1), piece, h), f32),
            pltpu.VMEM((outer, piece, h), f32),
            pltpu.VMEM((3 * h, h), f32),
            pltpu.VMEM((k, width), f32),
            pltpu.VMEM((max(inner - 1, 1), xp, width), f32),
            pltpu.VMEM((xp, width), f32),
            pltpu.VMEM(mid_in, f32),
            pltpu.VMEM((k, width), f32),
            pltpu.SemaphoreType.DMA((2, steps)),
            pltpu.SemaphoreType.DMA((2, g_copies)),
            pltpu.SemaphoreType.DMA((2, x_copies)),
            pltpu.SemaphoreType.DMA((2,)),
        ],
        compiler_params=pltpu.CompilerParams(collective_id=0, has_side_effects=True),
        cost_estimate=pl.CostEstimate(flops=2 * m * k * (k + width), bytes_accessed=2 * m * (k + width), transcendentals=0),
        name="sums",
    )(panel, slab)


def finish_kernel(cross_ref, invt_ref, panel_ref, slab_ref, coupling_ref, out_ref, update_ref):
    @pl.when(pl.program_id(0) == 0)
    def _():
        coupling = mm(invt_ref[...], cross_ref[...])
        coupling_ref[...] = coupling
        update_ref[...] = mm(invt_ref[...], coupling, 0, 0).astype(jnp.bfloat16)

    taken = jnp.dot(panel_ref[...], update_ref[...], preferred_element_type=jnp.float32)
    out_ref[...] = (slab_ref[...].astype(jnp.float32) - taken).astype(jnp.bfloat16)


def finish(cross, invt, panel, slab):
    m, k = panel.shape
    width = slab.shape[1]
    rows = m // 8
    whole = lambda i: (0, 0)
    part = lambda i: (i, 0)
    return pl.pallas_call(
        finish_kernel,
        grid=(m // rows,),
        out_shape=(jax.ShapeDtypeStruct((k, width), jnp.float32), jax.ShapeDtypeStruct((m, width), jnp.bfloat16)),
        in_specs=[
            pl.BlockSpec((k, width), whole),
            pl.BlockSpec((k, k), whole),
            pl.BlockSpec((rows, k), part),
            pl.BlockSpec((rows, width), part),
        ],
        out_specs=[pl.BlockSpec((k, width), whole), pl.BlockSpec((rows, width), part)],
        scratch_shapes=[pltpu.VMEM((k, width), jnp.bfloat16)],
        cost_estimate=pl.CostEstimate(flops=2 * m * k * width, bytes_accessed=2 * m * (k + 2 * width), transcendentals=0),
        name="finish",
    )(cross, invt, panel, slab)


def on_device(panel, slab):
    rows, cols = lax.axis_size("row"), lax.axis_size("col")
    gram, cross = sums(panel, slab, rows, cols)
    factor, invt = factor_and_invt(gram)
    coupling, remainder = finish(cross, invt, panel, slab)
    share = factor.shape[1] // cols
    factor_part = lax.dynamic_slice_in_dim(factor, lax.axis_index("col") * share, share, 1)
    return (factor_part, coupling, remainder)


def solution(mesh):
    from jax.sharding import PartitionSpec as P

    return jax.shard_map(
        on_device,
        mesh=mesh,
        in_specs=(P("row", None), P("row", "col")),
        out_specs=(P(None, "col"), P(None, "col"), P("row", "col")),
        check_vma=False,
    )
```

```python
import functools

import jax
import jax.numpy as jnp
from jax import lax
from jax.experimental import pallas as pl
from jax.experimental.pallas import tpu as pltpu

HI = lax.Precision.HIGHEST
MESH = pl.DeviceIdType.MESH


def mm(a, b, ca=1, cb=0):
    return lax.dot_general(a, b, (((ca,), (cb,)), ((), ())), precision=HI, preferred_element_type=jnp.float32)


def row_of(x, s):
    return jnp.broadcast_to(x[s : s + 1, :], x.shape)


def lane_of(x, i):
    return jnp.broadcast_to(x[:, i : i + 1], x.shape)


def split3(x):
    hi = x.astype(jnp.bfloat16)
    rest = x - hi.astype(jnp.float32)
    mid = rest.astype(jnp.bfloat16)
    low = (rest - mid.astype(jnp.float32)).astype(jnp.bfloat16)
    return hi, mid, low


def outer(a, b):
    ah, am, al = split3(a)
    bh, bm, bl = split3(b)
    left = jnp.concatenate([ah, ah, am, ah, al, am], axis=0)
    right = jnp.concatenate([bh, bm, bh, bl, bh, bm], axis=0)
    return lax.dot_general(left, right, (((0,), (0,)), ((), ())), preferred_element_type=jnp.float32)


BLOCK, STEP, TILE = 32, 16, 128


def eliminate(m_ref, r_ref, w_ref, b):
    n = m_ref.shape[1]
    groups = BLOCK // 8
    shape = (8, TILE)
    sub = lax.broadcasted_iota(jnp.int32, shape, 0)
    lane = lax.broadcasted_iota(jnp.int32, shape, 1)
    top = b * BLOCK
    t, lo = top // TILE, top % TILE
    tiles = n // TILE
    inside = (lane >= lo) & (lane < lo + BLOCK)

    def rows(u):
        return [m_ref[top + 8 * g : top + 8 * g + 8, u * TILE : (u + 1) * TILE] for g in range(groups)]

    own = rows(t)
    unit = [jnp.where(inside, jnp.where(lane == sub + (lo + 8 * g), 1.0, 0.0), own[g]) for g in range(groups)]
    other = {u: rows(u) for u in range(tiles) if u != t}
    slabs = [own, unit] + list(other.values())
    for first in range(0, BLOCK, STEP):
        c = [{g: lane_of(own[g], lo + first + k) for g in range((first + k) // 8, groups)} for k in range(STEP)]
        for k in range(STEP):
            gj, sj = divmod(first + k, 8)
            inv = lax.rsqrt(row_of(c[k][gj], sj))
            l = {g: c[k][g] * inv for g in range(gj, groups)}
            for k2 in range(k + 1, STEP):
                g2, s2 = divmod(first + k2, 8)
                at = row_of(l[g2], s2)
                for g in range(g2, groups):
                    c[k2][g] = c[k2][g] - l[g] * at
            below = jnp.where(sub > sj, l[gj], 0.0)
            for x in slabs:
                pivot = row_of(x[gj], sj) * inv
                x[gj] = jnp.where(sub == sj, pivot, x[gj] - below * pivot)
                for g in range(gj + 1, groups):
                    x[g] = x[g] - l[g] * pivot
    zero = jnp.zeros(shape, jnp.float32)
    for g in range(groups):
        at = pl.ds(top + 8 * g, 8)
        for u in range(tiles):
            cols = pl.ds(u * TILE, TILE)
            if u == t:
                r_ref[at, cols] = jnp.where(lane >= sub + (lo + 8 * g), own[g], 0.0)
                w_ref[at, cols] = jnp.where(lane < lo + BLOCK, unit[g], 0.0)
            else:
                r_ref[at, cols] = other[u][g] if u > t else zero
                w_ref[at, cols] = other[u][g] if u < t else zero
    end = top + BLOCK
    if end < n:
        done = jnp.concatenate(
            [jnp.concatenate([unit[g] if u == t else other[u][g] for u in range(tiles)], axis=1) for g in range(groups)], axis=0
        )
        skip = (end // TILE) * TILE
        taken = outer(done[:, skip:], done)
        for u in range(tiles):
            cols = slice(u * TILE, (u + 1) * TILE)
            old = m_ref[end:, cols]
            if u == t:
                wide = lax.broadcasted_iota(jnp.int32, old.shape, 1)
                old = jnp.where((wide >= lo) & (wide < lo + BLOCK), 0.0, old)
            m_ref[end:, cols] = old - taken[end - skip :, cols]


def factor_kernel(sliced, gram_ref, part_ref, invt_ref, m_ref, r_ref):
    h = gram_ref.shape[1]
    m_ref[:h, :h] = gram_ref[:h, :]
    m_ref[:h, h:] = gram_ref[h : 2 * h, :]
    m_ref[h:, h:] = gram_ref[2 * h :, :]
    m_ref[h:, :h] = jnp.zeros((h, h), jnp.float32)
    for b in range(m_ref.shape[0] // BLOCK):
        eliminate(m_ref, r_ref, invt_ref, b)
    share = part_ref.shape[1]
    if sliced:
        part_ref[...] = r_ref[:, pl.ds(pl.multiple_of(lax.axis_index("col") * share, TILE), share)]
    else:
        part_ref[...] = r_ref[...]


def factor_and_invt(blocks, cols):
    h = blocks.shape[1]
    n = 2 * h
    f32 = jnp.float32
    sliced = (n // cols) % TILE == 0
    part, invt = pl.pallas_call(
        functools.partial(factor_kernel, sliced),
        out_shape=(jax.ShapeDtypeStruct((n, n // cols if sliced else n), f32), jax.ShapeDtypeStruct((n, n), f32)),
        scratch_shapes=[pltpu.VMEM((n, n), f32), pltpu.VMEM((n, n), f32)],
        cost_estimate=pl.CostEstimate(flops=60_000_000, bytes_accessed=3 * n * n * 4, transcendentals=n),
        name="factor",
    )(blocks)
    if not sliced:
        part = lax.dynamic_slice_in_dim(part, lax.axis_index("col") * (n // cols), n // cols, 1)
    return part, invt


def levels(rows):
    inner = 1
    while inner * inner * 4 <= rows:
        inner *= 2
    return inner, rows // inner


def sums_kernel(
    inner, outer, cols, split, scale,
    panel_hbm, slab_hbm, gram_out, cross_out,
    panel, slab, g_own, g_in, g_mid, g_all, x_own, x_in, x_mid, x_mid_in, x_all,
    load_sem, g_sem, x_sem, out_sem,
):
    row = lax.axis_index("row")
    col = lax.axis_index("col")
    high, low = row // inner, row % inner
    f32 = jnp.float32

    def near(d):
        return high * inner + (low + d) % inner

    def far(d):
        return ((high + d) % outer) * inner + low

    chunks = panel.shape[0] // load_sem.shape[1]
    steps = load_sem.shape[1]
    loads = []
    for t in range(steps):
        part = pl.ds(t * chunks, chunks)
        loads.append(pltpu.make_async_copy(panel_hbm.at[part], panel.at[part], load_sem.at[0, t]))
    for t in range(steps):
        part = pl.ds(t * chunks, chunks)
        loads.append(pltpu.make_async_copy(slab_hbm.at[part], slab.at[part], load_sem.at[1, t]))
    for copy in loads:
        copy.start()

    barrier = pltpu.get_barrier_semaphore()
    greeted = 0
    for d in range(inner):
        for e in range(cols if split > 1 else 1):
            if d or e:
                pl.semaphore_signal(barrier, 1, device_id={"row": near(d), "col": (col + e) % cols}, device_id_type=MESH)
                greeted += 1
    for d in range(1, outer):
        pl.semaphore_signal(barrier, 1, device_id={"row": far(d), "col": col}, device_id_type=MESH)
        greeted += 1

    def send(src, dst, sems, index, to_row, to_col):
        copy = pltpu.make_async_remote_copy(
            src_ref=src, dst_ref=dst, send_sem=sems.at[0, index], recv_sem=sems.at[1, index],
            device_id={"row": to_row, "col": to_col}, device_id_type=MESH,
        )
        copy.start()
        return copy

    def tdot(a, b):
        return lax.dot_general(a, b, (((0,), (0,)), ((), ())), preferred_element_type=f32)

    h = g_own.shape[1]
    acc = None
    for t in range(steps):
        loads[t].wait()
        p = panel[t * chunks : (t + 1) * chunks, :]
        term = tdot(p, p)
        acc = term if acc is None else acc + term
    acc = acc * scale
    g_own[:h, :] = acc[:h, :h]
    g_own[h : 2 * h, :] = acc[:h, h:]
    g_own[2 * h :, :] = acc[h:, h:]

    pl.semaphore_wait(barrier, greeted)

    share = g_own.shape[0] // split
    piece = share // inner
    base = (col * share) if split > 1 else 0
    g1 = []
    for d in range(1, inner):
        at = pl.multiple_of(base + ((low + d) % inner) * piece, 8)
        g1.append(send(g_own.at[pl.ds(at, piece)], g_in.at[d - 1], g_sem, d - 1, near(d), col))
    used = inner - 1

    acc = None
    for t in range(steps):
        loads[steps + t].wait()
        term = tdot(panel[t * chunks : (t + 1) * chunks, :], slab[t * chunks : (t + 1) * chunks, :])
        acc = term if acc is None else acc + term
    x_own[...] = acc * scale

    xp = x_own.shape[0] // inner
    x1 = []
    for d in range(1, inner):
        at = pl.multiple_of(((low + d) % inner) * xp, 8)
        x1.append(send(x_own.at[pl.ds(at, xp)], x_in.at[d - 1], x_sem, d - 1, near(d), col))
    xused = inner - 1

    mine = pl.multiple_of(base + low * piece, 8)
    total = g_own[pl.ds(mine, piece), :]
    for d in range(1, inner):
        g1[d - 1].wait()
        total = total + g_in[d - 1]
    g_mid[high] = total
    g2 = []
    for d in range(1, outer):
        g2.append(send(g_mid.at[high], g_mid.at[high], g_sem, used + d - 1, far(d), col))
    used += outer - 1
    for copy in g2:
        copy.wait()
    total = g_mid[0]
    for q in range(1, outer):
        total = total + g_mid[q]
    g_all[pl.ds(mine, piece), :] = total
    g3 = []
    for d in range(inner):
        for e in range(cols if split > 1 else 1):
            if d or e:
                part = g_all.at[pl.ds(mine, piece)]
                g3.append(send(part, part, g_sem, used, near(d), (col + e) % cols))
                used += 1

    at = pl.multiple_of(low * xp, 8)
    total = x_own[pl.ds(at, xp), :]
    for d in range(1, inner):
        x1[d - 1].wait()
        total = total + x_in[d - 1]
    xq = xp // outer
    if xq % 8 == 0:
        x_mid[...] = total
        x2 = []
        for d in range(1, outer):
            there = pl.multiple_of(((high + d) % outer) * xq, 8)
            x2.append(send(x_mid.at[pl.ds(there, xq)], x_mid_in.at[d - 1], x_sem, xused + d - 1, far(d), col))
        xused += outer - 1
        here = pl.multiple_of(high * xq, 8)
        total = x_mid[pl.ds(here, xq), :]
        for d in range(1, outer):
            x2[d - 1].wait()
            total = total + x_mid_in[d - 1]
        spot = pl.multiple_of(low * xp + high * xq, 8)
        x_all[pl.ds(spot, xq), :] = total
        x3 = []
        for d in range(1, outer):
            part = x_all.at[pl.ds(spot, xq)]
            x3.append(send(part, part, x_sem, xused + d - 1, far(d), col))
        xused += outer - 1
        for copy in x3:
            copy.wait()
    else:
        x_mid_in[high] = total
        x2 = []
        for d in range(1, outer):
            x2.append(send(x_mid_in.at[high], x_mid_in.at[high], x_sem, xused + d - 1, far(d), col))
        xused += outer - 1
        for copy in x2:
            copy.wait()
        total = x_mid_in[0]
        for q in range(1, outer):
            total = total + x_mid_in[q]
        x_all[pl.ds(at, xp), :] = total
    x4 = []
    for d in range(1, inner):
        part = x_all.at[pl.ds(at, xp)]
        x4.append(send(part, part, x_sem, xused + d - 1, near(d), col))

    for copy in g3:
        copy.wait()
    out = pltpu.make_async_copy(g_all, gram_out, out_sem.at[0])
    out.start()
    for copy in x4:
        copy.wait()
    out2 = pltpu.make_async_copy(x_all, cross_out, out_sem.at[1])
    out2.start()
    out.wait()
    out2.wait()


def sums(panel, slab, rows, cols):
    m, k = panel.shape
    width = slab.shape[1]
    inner, outer = levels(rows)
    h = k // 2
    split = cols if (3 * h) % (8 * inner * cols) == 0 else 1
    piece = 3 * h // split // inner
    xp = k // inner
    xq = xp // outer
    f32 = jnp.float32
    mid_in = (max(outer - 1, 1), xq, width) if xq % 8 == 0 else (outer, xp, width)
    g_copies = (inner - 1) + (outer - 1) + inner * (cols if split > 1 else 1) - 1
    x_copies = 2 * (inner - 1) + 2 * (outer - 1)
    steps = 4
    any_space = pl.BlockSpec(memory_space=pl.ANY)
    return pl.pallas_call(
        functools.partial(sums_kernel, inner, outer, cols, split, 1.0 / (m * rows)),
        out_shape=(jax.ShapeDtypeStruct((3 * h, h), f32), jax.ShapeDtypeStruct((k, width), f32)),
        in_specs=[any_space, any_space],
        out_specs=[any_space, any_space],
        scratch_shapes=[
            pltpu.VMEM((m, k), panel.dtype),
            pltpu.VMEM((m, width), slab.dtype),
            pltpu.VMEM((3 * h, h), f32),
            pltpu.VMEM((max(inner - 1, 1), piece, h), f32),
            pltpu.VMEM((outer, piece, h), f32),
            pltpu.VMEM((3 * h, h), f32),
            pltpu.VMEM((k, width), f32),
            pltpu.VMEM((max(inner - 1, 1), xp, width), f32),
            pltpu.VMEM((xp, width), f32),
            pltpu.VMEM(mid_in, f32),
            pltpu.VMEM((k, width), f32),
            pltpu.SemaphoreType.DMA((2, steps)),
            pltpu.SemaphoreType.DMA((2, g_copies)),
            pltpu.SemaphoreType.DMA((2, x_copies)),
            pltpu.SemaphoreType.DMA((2,)),
        ],
        compiler_params=pltpu.CompilerParams(collective_id=0, has_side_effects=True),
        cost_estimate=pl.CostEstimate(flops=2 * m * k * (k + width), bytes_accessed=2 * m * (k + width), transcendentals=0),
        name="sums",
    )(panel, slab)


def finish_kernel(cross_ref, invt_ref, panel_ref, slab_ref, coupling_ref, out_ref, update_ref):
    @pl.when(pl.program_id(0) == 0)
    def _():
        coupling = mm(invt_ref[...], cross_ref[...])
        coupling_ref[...] = coupling
        update_ref[...] = mm(invt_ref[...], coupling, 0, 0).astype(jnp.bfloat16)

    taken = jnp.dot(panel_ref[...], update_ref[...], preferred_element_type=jnp.float32)
    out_ref[...] = (slab_ref[...].astype(jnp.float32) - taken).astype(jnp.bfloat16)


def finish(cross, invt, panel, slab):
    m, k = panel.shape
    width = slab.shape[1]
    rows = m // 8
    whole = lambda i: (0, 0)
    part = lambda i: (i, 0)
    return pl.pallas_call(
        finish_kernel,
        grid=(m // rows,),
        out_shape=(jax.ShapeDtypeStruct((k, width), jnp.float32), jax.ShapeDtypeStruct((m, width), jnp.bfloat16)),
        in_specs=[
            pl.BlockSpec((k, width), whole),
            pl.BlockSpec((k, k), whole),
            pl.BlockSpec((rows, k), part),
            pl.BlockSpec((rows, width), part),
        ],
        out_specs=[pl.BlockSpec((k, width), whole), pl.BlockSpec((rows, width), part)],
        scratch_shapes=[pltpu.VMEM((k, width), jnp.bfloat16)],
        cost_estimate=pl.CostEstimate(flops=2 * m * k * width, bytes_accessed=2 * m * (k + 2 * width), transcendentals=0),
        name="finish",
    )(cross, invt, panel, slab)


def on_device(panel, slab):
    rows, cols = lax.axis_size("row"), lax.axis_size("col")
    gram, cross = sums(panel, slab, rows, cols)
    factor_part, invt = factor_and_invt(gram, cols)
    coupling, remainder = finish(cross, invt, panel, slab)
    return (factor_part, coupling, remainder)


def solution(mesh):
    from jax.sharding import PartitionSpec as P

    return jax.shard_map(
        on_device,
        mesh=mesh,
        in_specs=(P("row", None), P("row", "col")),
        out_specs=(P(None, "col"), P(None, "col"), P("row", "col")),
        check_vma=False,
    )
```

```python
import functools

import jax
import jax.numpy as jnp
from jax import lax
from jax.experimental import pallas as pl
from jax.experimental.pallas import tpu as pltpu

HI = lax.Precision.HIGHEST
MESH = pl.DeviceIdType.MESH


def mm(a, b, ca=1, cb=0):
    return lax.dot_general(a, b, (((ca,), (cb,)), ((), ())), precision=HI, preferred_element_type=jnp.float32)


def row_of(x, s):
    return jnp.broadcast_to(x[s : s + 1, :], x.shape)


def lane_of(x, i):
    return jnp.broadcast_to(x[:, i : i + 1], x.shape)


def split3(x):
    hi = x.astype(jnp.bfloat16)
    rest = x - hi.astype(jnp.float32)
    mid = rest.astype(jnp.bfloat16)
    low = (rest - mid.astype(jnp.float32)).astype(jnp.bfloat16)
    return hi, mid, low


def outer(a, b):
    ah, am, al = split3(a)
    bh, bm, bl = split3(b)
    left = jnp.concatenate([ah, ah, am, ah, al, am], axis=0)
    right = jnp.concatenate([bh, bm, bh, bl, bh, bm], axis=0)
    return lax.dot_general(left, right, (((0,), (0,)), ((), ())), preferred_element_type=jnp.float32)


BLOCK, STEP, TILE = 32, 16, 128


def eliminate(m_ref, r_ref, w_ref, b):
    n = m_ref.shape[1]
    groups = BLOCK // 8
    shape = (8, TILE)
    sub = lax.broadcasted_iota(jnp.int32, shape, 0)
    lane = lax.broadcasted_iota(jnp.int32, shape, 1)
    top = b * BLOCK
    t, lo = top // TILE, top % TILE
    tiles = n // TILE
    inside = (lane >= lo) & (lane < lo + BLOCK)

    def rows(u):
        return [m_ref[top + 8 * g : top + 8 * g + 8, u * TILE : (u + 1) * TILE] for g in range(groups)]

    own = rows(t)
    unit = [jnp.where(inside, jnp.where(lane == sub + (lo + 8 * g), 1.0, 0.0), own[g]) for g in range(groups)]
    other = {u: rows(u) for u in range(tiles) if u != t}
    slabs = [own, unit] + list(other.values())
    for first in range(0, BLOCK, STEP):
        c = [{g: lane_of(own[g], lo + first + k) for g in range((first + k) // 8, groups)} for k in range(STEP)]
        for k in range(STEP):
            gj, sj = divmod(first + k, 8)
            inv = lax.rsqrt(row_of(c[k][gj], sj))
            l = {g: c[k][g] * inv for g in range(gj, groups)}
            for k2 in range(k + 1, STEP):
                g2, s2 = divmod(first + k2, 8)
                at = row_of(l[g2], s2)
                for g in range(g2, groups):
                    c[k2][g] = c[k2][g] - l[g] * at
            below = jnp.where(sub > sj, l[gj], 0.0)
            for x in slabs:
                pivot = row_of(x[gj], sj) * inv
                x[gj] = jnp.where(sub == sj, pivot, x[gj] - below * pivot)
                for g in range(gj + 1, groups):
                    x[g] = x[g] - l[g] * pivot
    zero = jnp.zeros(shape, jnp.float32)
    for g in range(groups):
        at = pl.ds(top + 8 * g, 8)
        for u in range(tiles):
            cols = pl.ds(u * TILE, TILE)
            if u == t:
                r_ref[at, cols] = jnp.where(lane >= sub + (lo + 8 * g), own[g], 0.0)
                w_ref[at, cols] = jnp.where(lane < lo + BLOCK, unit[g], 0.0)
            else:
                r_ref[at, cols] = other[u][g] if u > t else zero
                w_ref[at, cols] = other[u][g] if u < t else zero
    end = top + BLOCK
    if end < n:
        done = jnp.concatenate(
            [jnp.concatenate([unit[g] if u == t else other[u][g] for u in range(tiles)], axis=1) for g in range(groups)], axis=0
        )
        skip = (end // TILE) * TILE
        taken = outer(done[:, skip:], done)
        for u in range(tiles):
            cols = slice(u * TILE, (u + 1) * TILE)
            old = m_ref[end:, cols]
            if u == t:
                wide = lax.broadcasted_iota(jnp.int32, old.shape, 1)
                old = jnp.where((wide >= lo) & (wide < lo + BLOCK), 0.0, old)
            m_ref[end:, cols] = old - taken[end - skip :, cols]


def levels(rows):
    inner = 1
    while inner * inner * 4 <= rows:
        inner *= 2
    return inner, rows // inner


def send(src, dst, sems, index, to_row, to_col):
    copy = pltpu.make_async_remote_copy(
        src_ref=src, dst_ref=dst, send_sem=sems.at[0, index], recv_sem=sems.at[1, index],
        device_id={"row": to_row, "col": to_col}, device_id_type=MESH,
    )
    copy.start()
    return copy


def reduce_all(own, first_in, mid, second_in, result, sems, first, second, col):
    (na, ia, pa), (nb, ib, pb) = first, second
    ra = own.shape[0] // na
    rb = ra // nb
    used = 0

    def to(d, level, src, dst):
        nonlocal used
        used += 1
        return send(src, dst, sems, used - 1, level(d), col)

    sent = []
    for d in range(1, na):
        at = pl.multiple_of(((ia + d) % na) * ra, 8)
        sent.append(to(d, pa, own.at[pl.ds(at, ra)], first_in.at[d - 1]))
    yield
    here = pl.multiple_of(ia * ra, 8)
    total = own[pl.ds(here, ra), :]
    for d in range(1, na):
        sent[d - 1].wait()
        total = total + first_in[d - 1]
    sent = []
    if rb % 8 == 0:
        mid[...] = total
        for d in range(1, nb):
            at = pl.multiple_of(((ib + d) % nb) * rb, 8)
            sent.append(to(d, pb, mid.at[pl.ds(at, rb)], second_in.at[d - 1]))
        yield
        total = mid[pl.ds(pl.multiple_of(ib * rb, 8), rb), :]
        for d in range(1, nb):
            sent[d - 1].wait()
            total = total + second_in[d - 1]
        spot = pl.multiple_of(ia * ra + ib * rb, 8)
        result[pl.ds(spot, rb), :] = total
        sent = []
        for d in range(1, nb):
            part = result.at[pl.ds(spot, rb)]
            sent.append(to(d, pb, part, part))
        yield
        for copy in sent:
            copy.wait()
    else:
        second_in[ib] = total
        for d in range(1, nb):
            sent.append(to(d, pb, second_in.at[ib], second_in.at[ib]))
        yield
        for copy in sent:
            copy.wait()
        total = second_in[0]
        for q in range(1, nb):
            total = total + second_in[q]
        result[pl.ds(here, ra), :] = total
        yield
    sent = []
    for d in range(1, na):
        part = result.at[pl.ds(here, ra)]
        sent.append(to(d, pa, part, part))
    yield
    for copy in sent:
        copy.wait()
    yield


def reduce_scratch(k, width, na, nb):
    f32 = jnp.float32
    ra = k // na
    rb = ra // nb
    second_in = (max(nb - 1, 1), rb, width) if rb % 8 == 0 else (nb, ra, width)
    return [
        pltpu.VMEM((k, width), f32),
        pltpu.VMEM((max(na - 1, 1), ra, width), f32),
        pltpu.VMEM((ra, width), f32),
        pltpu.VMEM(second_in, f32),
        pltpu.VMEM((k, width), f32),
        pltpu.SemaphoreType.DMA((2, 2 * (na - 1) + 2 * (nb - 1))),
    ]


def product(w, x, ca):
    wh, wm, wl = split3(w)
    xh, xm, xl = split3(x)
    left = jnp.concatenate([wh, wh, wm, wh, wl, wm], axis=ca)
    right = jnp.concatenate([xh, xm, xh, xl, xh, xm], axis=0)
    return lax.dot_general(left, right, (((ca,), (0,)), ((), ())), preferred_element_type=jnp.float32)


def solve_kernel(
    inner, outer_, cols, split, scale, widths, sliced,
    panel_hbm, slab_hbm, part_out, coupling_out, update_out,
    panel, slab, g_own, g_in, g_mid, g_all, m_ref, r_ref, w_ref, part, coupling, update,
    load_sem, g_sem, out_sem, *cross_refs,
):
    row = lax.axis_index("row")
    col = lax.axis_index("col")
    high, low = row // inner, row % inner
    f32 = jnp.float32
    all_cols = range(cols if split > 1 else 1)

    def near(d):
        return high * inner + (low + d) % inner

    def far(d):
        return ((high + d) % outer_) * inner + low

    steps = load_sem.shape[1]
    chunk = panel.shape[0] // steps
    loads = []
    for which, (src, dst) in enumerate(((panel_hbm, panel), (slab_hbm, slab))):
        for t in range(steps):
            at = pl.ds(t * chunk, chunk)
            loads.append(pltpu.make_async_copy(src.at[at], dst.at[at], load_sem.at[which, t]))
    for copy in loads:
        copy.start()

    barrier = pltpu.get_barrier_semaphore()
    greeted = 0
    for d in range(inner):
        for e in all_cols:
            if d or e:
                pl.semaphore_signal(barrier, 1, device_id={"row": near(d), "col": (col + e) % cols}, device_id_type=MESH)
                greeted += 1
    for d in range(1, outer_):
        pl.semaphore_signal(barrier, 1, device_id={"row": far(d), "col": col}, device_id_type=MESH)
        greeted += 1

    def tdot(a, b):
        return lax.dot_general(a, b, (((0,), (0,)), ((), ())), preferred_element_type=f32)

    h = g_own.shape[1]
    acc = None
    for t in range(steps):
        loads[t].wait()
        p = panel[t * chunk : (t + 1) * chunk, :]
        term = tdot(p, p)
        acc = term if acc is None else acc + term
    acc = acc * scale
    g_own[:h, :] = acc[:h, :h]
    g_own[h : 2 * h, :] = acc[:h, h:]
    g_own[2 * h :, :] = acc[h:, h:]

    pl.semaphore_wait(barrier, greeted)

    share = g_own.shape[0] // split
    piece = share // inner
    base = (col * share) if split > 1 else 0
    sent = []
    for d in range(1, inner):
        at = pl.multiple_of(base + ((low + d) % inner) * piece, 8)
        sent.append(send(g_own.at[pl.ds(at, piece)], g_in.at[d - 1], g_sem, d - 1, near(d), col))
    used = inner - 1

    acc = None
    for t in range(steps):
        loads[steps + t].wait()
        term = tdot(panel[t * chunk : (t + 1) * chunk, :], slab[t * chunk : (t + 1) * chunk, :])
        acc = term if acc is None else acc + term
    acc = acc * scale
    flows = []
    left = 0
    for i, width in enumerate(widths):
        refs = cross_refs[6 * i : 6 * i + 6]
        refs[0][...] = acc[:, left : left + width]
        left += width
        ends = ((inner, low, near), (outer_, high, far))
        flows.append(reduce_all(*refs, *(ends if i == 0 else ends[::-1]), col))

    def advance():
        for flow in flows:
            next(flow)

    advance()

    mine = pl.multiple_of(base + low * piece, 8)
    total = g_own[pl.ds(mine, piece), :]
    for d in range(1, inner):
        sent[d - 1].wait()
        total = total + g_in[d - 1]
    g_mid[high] = total
    sent = []
    for d in range(1, outer_):
        sent.append(send(g_mid.at[high], g_mid.at[high], g_sem, used, far(d), col))
        used += 1
    for copy in sent:
        copy.wait()
    total = g_mid[0]
    for q in range(1, outer_):
        total = total + g_mid[q]
    g_all[pl.ds(mine, piece), :] = total
    sent = []
    for d in range(inner):
        for e in all_cols:
            if d or e:
                at = g_all.at[pl.ds(mine, piece)]
                sent.append(send(at, at, g_sem, used, near(d), (col + e) % cols))
                used += 1
    advance()
    for copy in sent:
        copy.wait()

    m_ref[:h, :h] = g_all[:h, :]
    m_ref[:h, h:] = g_all[h : 2 * h, :]
    m_ref[h:, h:] = g_all[2 * h :, :]
    m_ref[h:, :h] = jnp.zeros((h, h), f32)
    count = m_ref.shape[0] // BLOCK
    for b in range(count):
        eliminate(m_ref, r_ref, w_ref, b)
        if b in (count // 4, (5 * count) // 8 + 1):
            advance()
    width = part.shape[1]
    if sliced:
        part[...] = r_ref[:, pl.ds(pl.multiple_of(col * width, TILE), width)]
    else:
        part[...] = r_ref[...]
    out = [pltpu.make_async_copy(part, part_out, out_sem.at[0])]
    out[0].start()
    advance()

    w = w_ref[...]
    cross = jnp.concatenate([cross_refs[6 * i + 4][...] for i in range(len(widths))], axis=1)
    x = product(w, cross, 1)
    coupling[...] = x
    out.append(pltpu.make_async_copy(coupling, coupling_out, out_sem.at[1]))
    out[1].start()
    update[...] = product(w, x, 0).astype(jnp.bfloat16)
    out.append(pltpu.make_async_copy(update, update_out, out_sem.at[2]))
    out[2].start()
    for copy in out:
        copy.wait()


def solve(panel, slab, rows, cols):
    m, k = panel.shape
    width = slab.shape[1]
    inner, outer_ = levels(rows)
    h = k // 2
    split = cols if (3 * h) % (8 * inner * cols) == 0 else 1
    piece = 3 * h // split // inner
    sliced = (k // cols) % TILE == 0
    share = k // cols if sliced else k
    f32, bf16 = jnp.float32, jnp.bfloat16
    ends = ((inner, outer_), (outer_, inner))
    quarter = width // 4
    widths = (width - quarter, quarter) if quarter % TILE == 0 and k % (8 * rows) == 0 else (width,)
    steps = 4
    g_copies = (inner - 1) + (outer_ - 1) + inner * (cols if split > 1 else 1) - 1
    hbm = pl.BlockSpec(memory_space=pl.ANY)
    scratch = [
        pltpu.VMEM((m, k), bf16),
        pltpu.VMEM((m, width), bf16),
        pltpu.VMEM((3 * h, h), f32),
        pltpu.VMEM((max(inner - 1, 1), piece, h), f32),
        pltpu.VMEM((outer_, piece, h), f32),
        pltpu.VMEM((3 * h, h), f32),
        pltpu.VMEM((k, k), f32),
        pltpu.VMEM((k, k), f32),
        pltpu.VMEM((k, k), f32),
        pltpu.VMEM((k, share), f32),
        pltpu.VMEM((k, width), f32),
        pltpu.VMEM((k, width), bf16),
        pltpu.SemaphoreType.DMA((2, steps)),
        pltpu.SemaphoreType.DMA((2, g_copies)),
        pltpu.SemaphoreType.DMA((3,)),
    ]
    for i, w in enumerate(widths):
        scratch += reduce_scratch(k, w, *ends[i])
    part, coupling, update = pl.pallas_call(
        functools.partial(solve_kernel, inner, outer_, cols, split, 1.0 / (m * rows), widths, sliced),
        out_shape=(
            jax.ShapeDtypeStruct((k, share), f32),
            jax.ShapeDtypeStruct((k, width), f32),
            jax.ShapeDtypeStruct((k, width), bf16),
        ),
        in_specs=[hbm, hbm],
        out_specs=[hbm, hbm, hbm],
        scratch_shapes=scratch,
        compiler_params=pltpu.CompilerParams(collective_id=0, has_side_effects=True),
        cost_estimate=pl.CostEstimate(flops=2 * m * k * (k + width), bytes_accessed=2 * m * (k + width), transcendentals=0),
        name="solve",
    )(panel, slab)
    if not sliced:
        part = lax.dynamic_slice_in_dim(part, lax.axis_index("col") * (k // cols), k // cols, 1)
    return part, coupling, update


def finish_kernel(part_ref, coupling_ref, update_ref, panel_ref, slab_ref, part_out, coupling_out, out_ref):
    @pl.when(pl.program_id(0) == 0)
    def _():
        part_out[...] = part_ref[...]
        coupling_out[...] = coupling_ref[...]

    taken = jnp.dot(panel_ref[...], update_ref[...], preferred_element_type=jnp.float32)
    out_ref[...] = (slab_ref[...].astype(jnp.float32) - taken).astype(jnp.bfloat16)


def finish(part, coupling, update, panel, slab):
    m, k = panel.shape
    width = slab.shape[1]
    rows = m // 8
    whole = lambda i: (0, 0)
    tile = lambda i: (i, 0)
    return pl.pallas_call(
        finish_kernel,
        grid=(m // rows,),
        out_shape=(
            jax.ShapeDtypeStruct(part.shape, part.dtype),
            jax.ShapeDtypeStruct(coupling.shape, coupling.dtype),
            jax.ShapeDtypeStruct((m, width), jnp.bfloat16),
        ),
        in_specs=[
            pl.BlockSpec(part.shape, whole),
            pl.BlockSpec((k, width), whole),
            pl.BlockSpec((k, width), whole),
            pl.BlockSpec((rows, k), tile),
            pl.BlockSpec((rows, width), tile),
        ],
        out_specs=[pl.BlockSpec(part.shape, whole), pl.BlockSpec((k, width), whole), pl.BlockSpec((rows, width), tile)],
        cost_estimate=pl.CostEstimate(flops=2 * m * k * width, bytes_accessed=2 * m * (k + 2 * width), transcendentals=0),
        name="finish",
    )(part, coupling, update, panel, slab)


def on_device(panel, slab):
    rows, cols = lax.axis_size("row"), lax.axis_size("col")
    part, coupling, update = solve(panel, slab, rows, cols)
    return finish(part, coupling, update, panel, slab)


def solution(mesh):
    from jax.sharding import PartitionSpec as P

    return jax.shard_map(
        on_device,
        mesh=mesh,
        in_specs=(P("row", None), P("row", "col")),
        out_specs=(P(None, "col"), P(None, "col"), P("row", "col")),
        check_vma=False,
    )
```

```python
import functools

import jax
import jax.numpy as jnp
from jax import lax
from jax.experimental import pallas as pl
from jax.experimental.pallas import tpu as pltpu

HI = lax.Precision.HIGHEST
MESH = pl.DeviceIdType.MESH


def mm(a, b, ca=1, cb=0):
    return lax.dot_general(a, b, (((ca,), (cb,)), ((), ())), precision=HI, preferred_element_type=jnp.float32)


def row_of(x, s):
    return jnp.broadcast_to(x[s : s + 1, :], x.shape)


def lane_of(x, i):
    return jnp.broadcast_to(x[:, i : i + 1], x.shape)


def split3(x):
    hi = x.astype(jnp.bfloat16)
    rest = x - hi.astype(jnp.float32)
    mid = rest.astype(jnp.bfloat16)
    low = (rest - mid.astype(jnp.float32)).astype(jnp.bfloat16)
    return hi, mid, low


def outer(a, b):
    ah, am, al = split3(a)
    bh, bm, bl = split3(b)
    left = jnp.concatenate([ah, ah, am, ah, al, am], axis=0)
    right = jnp.concatenate([bh, bm, bh, bl, bh, bm], axis=0)
    return lax.dot_general(left, right, (((0,), (0,)), ((), ())), preferred_element_type=jnp.float32)


BLOCK, STEP, TILE = 32, 16, 128


def eliminate(m_ref, r_ref, w_ref, b):
    n = m_ref.shape[1]
    groups = BLOCK // 8
    shape = (8, TILE)
    sub = lax.broadcasted_iota(jnp.int32, shape, 0)
    lane = lax.broadcasted_iota(jnp.int32, shape, 1)
    top = b * BLOCK
    t, lo = top // TILE, top % TILE
    tiles = n // TILE
    inside = (lane >= lo) & (lane < lo + BLOCK)

    def rows(u):
        return [m_ref[top + 8 * g : top + 8 * g + 8, u * TILE : (u + 1) * TILE] for g in range(groups)]

    own = rows(t)
    unit = [jnp.where(inside, jnp.where(lane == sub + (lo + 8 * g), 1.0, 0.0), own[g]) for g in range(groups)]
    other = {u: rows(u) for u in range(tiles) if u != t}
    slabs = [own, unit] + list(other.values())
    for first in range(0, BLOCK, STEP):
        c = [{g: lane_of(own[g], lo + first + k) for g in range((first + k) // 8, groups)} for k in range(STEP)]
        for k in range(STEP):
            gj, sj = divmod(first + k, 8)
            inv = lax.rsqrt(row_of(c[k][gj], sj))
            l = {g: c[k][g] * inv for g in range(gj, groups)}
            for k2 in range(k + 1, STEP):
                g2, s2 = divmod(first + k2, 8)
                at = row_of(l[g2], s2)
                for g in range(g2, groups):
                    c[k2][g] = c[k2][g] - l[g] * at
            below = jnp.where(sub > sj, l[gj], 0.0)
            for x in slabs:
                pivot = row_of(x[gj], sj) * inv
                x[gj] = jnp.where(sub == sj, pivot, x[gj] - below * pivot)
                for g in range(gj + 1, groups):
                    x[g] = x[g] - l[g] * pivot
    zero = jnp.zeros(shape, jnp.float32)
    for g in range(groups):
        at = pl.ds(top + 8 * g, 8)
        for u in range(tiles):
            cols = pl.ds(u * TILE, TILE)
            if u == t:
                r_ref[at, cols] = jnp.where(lane >= sub + (lo + 8 * g), own[g], 0.0)
                w_ref[at, cols] = jnp.where(lane < lo + BLOCK, unit[g], 0.0)
            else:
                r_ref[at, cols] = other[u][g] if u > t else zero
                w_ref[at, cols] = other[u][g] if u < t else zero
    end = top + BLOCK
    if end < n:
        done = jnp.concatenate(
            [jnp.concatenate([unit[g] if u == t else other[u][g] for u in range(tiles)], axis=1) for g in range(groups)], axis=0
        )
        skip = (end // TILE) * TILE
        taken = outer(done[:, skip:], done)
        for u in range(tiles):
            cols = slice(u * TILE, (u + 1) * TILE)
            old = m_ref[end:, cols]
            if u == t:
                wide = lax.broadcasted_iota(jnp.int32, old.shape, 1)
                old = jnp.where((wide >= lo) & (wide < lo + BLOCK), 0.0, old)
            m_ref[end:, cols] = old - taken[end - skip :, cols]


def levels(rows):
    inner = 1
    while inner * inner * 4 <= rows:
        inner *= 2
    return inner, rows // inner


def send(src, dst, sems, index, to_row, to_col):
    copy = pltpu.make_async_remote_copy(
        src_ref=src, dst_ref=dst, send_sem=sems.at[0, index], recv_sem=sems.at[1, index],
        device_id={"row": to_row, "col": to_col}, device_id_type=MESH,
    )
    copy.start()
    return copy


def reduce_all(own, first_in, mid, second_in, result, sems, first, second, col):
    (na, ia, pa), (nb, ib, pb) = first, second
    ra = own.shape[0] // na
    rb = ra // nb
    used = 0

    def to(d, level, src, dst):
        nonlocal used
        used += 1
        return send(src, dst, sems, used - 1, level(d), col)

    sent = []
    for d in range(1, na):
        at = pl.multiple_of(((ia + d) % na) * ra, 8)
        sent.append(to(d, pa, own.at[pl.ds(at, ra)], first_in.at[d - 1]))
    yield
    here = pl.multiple_of(ia * ra, 8)
    total = own[pl.ds(here, ra), :]
    for d in range(1, na):
        sent[d - 1].wait()
        total = total + first_in[d - 1]
    sent = []
    if rb % 8 == 0:
        mid[...] = total
        for d in range(1, nb):
            at = pl.multiple_of(((ib + d) % nb) * rb, 8)
            sent.append(to(d, pb, mid.at[pl.ds(at, rb)], second_in.at[d - 1]))
        yield
        total = mid[pl.ds(pl.multiple_of(ib * rb, 8), rb), :]
        for d in range(1, nb):
            sent[d - 1].wait()
            total = total + second_in[d - 1]
        spot = pl.multiple_of(ia * ra + ib * rb, 8)
        result[pl.ds(spot, rb), :] = total
        sent = []
        for d in range(1, nb):
            part = result.at[pl.ds(spot, rb)]
            sent.append(to(d, pb, part, part))
        yield
        for copy in sent:
            copy.wait()
    else:
        second_in[ib] = total
        for d in range(1, nb):
            sent.append(to(d, pb, second_in.at[ib], second_in.at[ib]))
        yield
        for copy in sent:
            copy.wait()
        total = second_in[0]
        for q in range(1, nb):
            total = total + second_in[q]
        result[pl.ds(here, ra), :] = total
        yield
    sent = []
    for d in range(1, na):
        part = result.at[pl.ds(here, ra)]
        sent.append(to(d, pa, part, part))
    yield
    for copy in sent:
        copy.wait()
    yield


def reduce_scratch(k, width, na, nb):
    f32 = jnp.float32
    ra = k // na
    rb = ra // nb
    second_in = (max(nb - 1, 1), rb, width) if rb % 8 == 0 else (nb, ra, width)
    return [
        pltpu.VMEM((k, width), f32),
        pltpu.VMEM((max(na - 1, 1), ra, width), f32),
        pltpu.VMEM((ra, width), f32),
        pltpu.VMEM(second_in, f32),
        pltpu.VMEM((k, width), f32),
        pltpu.SemaphoreType.DMA((2, 2 * (na - 1) + 2 * (nb - 1))),
    ]


def product(w, x, ca):
    wh, wm, wl = split3(w)
    xh, xm, xl = split3(x)
    left = jnp.concatenate([wh, wh, wm, wh, wl, wm], axis=ca)
    right = jnp.concatenate([xh, xm, xh, xl, xh, xm], axis=0)
    return lax.dot_general(left, right, (((ca,), (0,)), ((), ())), preferred_element_type=jnp.float32)


def solve_kernel(
    inner, outer_, cols, split, scale, widths, sliced,
    panel_hbm, slab_hbm, part_out, coupling_out, update_out,
    panel, slab, g_own, g_in, g_mid, g_all, m_ref, r_ref, w_ref, part, coupling, update,
    load_sem, g_sem, out_sem, *cross_refs,
):
    row = lax.axis_index("row")
    col = lax.axis_index("col")
    high, low = row // inner, row % inner
    f32 = jnp.float32
    all_cols = range(cols if split > 1 else 1)

    def near(d):
        return high * inner + (low + d) % inner

    def far(d):
        return ((high + d) % outer_) * inner + low

    steps = load_sem.shape[1]
    chunk = panel.shape[0] // steps
    loads = []
    for which, (src, dst) in enumerate(((panel_hbm, panel), (slab_hbm, slab))):
        for t in range(steps):
            at = pl.ds(t * chunk, chunk)
            loads.append(pltpu.make_async_copy(src.at[at], dst.at[at], load_sem.at[which, t]))
    for copy in loads:
        copy.start()

    barrier = pltpu.get_barrier_semaphore()
    greeted = 0
    for d in range(inner):
        for e in all_cols:
            if d or e:
                pl.semaphore_signal(barrier, 1, device_id={"row": near(d), "col": (col + e) % cols}, device_id_type=MESH)
                greeted += 1
    for d in range(1, outer_):
        pl.semaphore_signal(barrier, 1, device_id={"row": far(d), "col": col}, device_id_type=MESH)
        greeted += 1

    def tdot(a, b):
        return lax.dot_general(a, b, (((0,), (0,)), ((), ())), preferred_element_type=f32)

    h = g_own.shape[1]
    acc = None
    for t in range(steps):
        loads[t].wait()
        p = panel[t * chunk : (t + 1) * chunk, :]
        term = tdot(p, p)
        acc = term if acc is None else acc + term
    acc = acc * scale
    g_own[:h, :] = acc[:h, :h]
    g_own[h : 2 * h, :] = acc[:h, h:]
    g_own[2 * h :, :] = acc[h:, h:]

    pl.semaphore_wait(barrier, greeted)

    share = g_own.shape[0] // split
    piece = share // inner
    base = (col * share) if split > 1 else 0
    sent = []
    for d in range(1, inner):
        at = pl.multiple_of(base + ((low + d) % inner) * piece, 8)
        sent.append(send(g_own.at[pl.ds(at, piece)], g_in.at[d - 1], g_sem, d - 1, near(d), col))
    used = inner - 1

    acc = None
    for t in range(steps):
        loads[steps + t].wait()
        term = tdot(panel[t * chunk : (t + 1) * chunk, :], slab[t * chunk : (t + 1) * chunk, :])
        acc = term if acc is None else acc + term
    acc = acc * scale
    flows = []
    left = 0
    for i, width in enumerate(widths):
        refs = cross_refs[6 * i : 6 * i + 6]
        refs[0][...] = acc[:, left : left + width]
        left += width
        ends = ((inner, low, near), (outer_, high, far))
        flows.append(reduce_all(*refs, *(ends if i == 0 else ends[::-1]), col))

    def advance():
        for flow in flows:
            next(flow)

    advance()

    mine = pl.multiple_of(base + low * piece, 8)
    total = g_own[pl.ds(mine, piece), :]
    for d in range(1, inner):
        sent[d - 1].wait()
        total = total + g_in[d - 1]
    g_mid[high] = total
    sent = []
    for d in range(1, outer_):
        sent.append(send(g_mid.at[high], g_mid.at[high], g_sem, used, far(d), col))
        used += 1
    for copy in sent:
        copy.wait()
    total = g_mid[0]
    for q in range(1, outer_):
        total = total + g_mid[q]
    g_all[pl.ds(mine, piece), :] = total
    sent = []
    for d in range(inner):
        for e in all_cols:
            if d or e:
                at = g_all.at[pl.ds(mine, piece)]
                sent.append(send(at, at, g_sem, used, near(d), (col + e) % cols))
                used += 1
    advance()
    for copy in sent:
        copy.wait()

    m_ref[:h, :h] = g_all[:h, :]
    m_ref[:h, h:] = g_all[h : 2 * h, :]
    m_ref[h:, h:] = g_all[2 * h :, :]
    m_ref[h:, :h] = jnp.zeros((h, h), f32)
    count = m_ref.shape[0] // BLOCK
    for b in range(count):
        eliminate(m_ref, r_ref, w_ref, b)
        if b in (count // 4, (5 * count) // 8 + 1):
            advance()
    width = part.shape[1]
    if sliced:
        part[...] = r_ref[:, pl.ds(pl.multiple_of(col * width, TILE), width)]
    else:
        part[...] = r_ref[...]
    out = [pltpu.make_async_copy(part, part_out, out_sem.at[0])]
    out[0].start()
    advance()

    w = w_ref[...]
    cross = jnp.concatenate([cross_refs[6 * i + 4][...] for i in range(len(widths))], axis=1)
    x = product(w, cross, 1)
    coupling[...] = x
    out.append(pltpu.make_async_copy(coupling, coupling_out, out_sem.at[1]))
    out[1].start()
    update[...] = product(w, x, 0).astype(jnp.bfloat16)
    out.append(pltpu.make_async_copy(update, update_out, out_sem.at[2]))
    out[2].start()
    for copy in out:
        copy.wait()


def solve(panel, slab, rows, cols):
    m, k = panel.shape
    width = slab.shape[1]
    inner, outer_ = levels(rows)
    h = k // 2
    split = cols if (3 * h) % (8 * inner * cols) == 0 else 1
    piece = 3 * h // split // inner
    sliced = (k // cols) % TILE == 0
    share = k // cols if sliced else k
    f32, bf16 = jnp.float32, jnp.bfloat16
    ends = ((inner, outer_), (outer_, inner))
    quarter = width // 4
    widths = (width - quarter, quarter) if quarter % TILE == 0 and k % (8 * rows) == 0 else (width,)
    steps = 4
    g_copies = (inner - 1) + (outer_ - 1) + inner * (cols if split > 1 else 1) - 1
    hbm = pl.BlockSpec(memory_space=pl.ANY)
    scratch = [
        pltpu.VMEM((m, k), bf16),
        pltpu.VMEM((m, width), bf16),
        pltpu.VMEM((3 * h, h), f32),
        pltpu.VMEM((max(inner - 1, 1), piece, h), f32),
        pltpu.VMEM((outer_, piece, h), f32),
        pltpu.VMEM((3 * h, h), f32),
        pltpu.VMEM((k, k), f32),
        pltpu.VMEM((k, k), f32),
        pltpu.VMEM((k, k), f32),
        pltpu.VMEM((k, share), f32),
        pltpu.VMEM((k, width), f32),
        pltpu.VMEM((k, width), bf16),
        pltpu.SemaphoreType.DMA((2, steps)),
        pltpu.SemaphoreType.DMA((2, g_copies)),
        pltpu.SemaphoreType.DMA((3,)),
    ]
    for i, w in enumerate(widths):
        scratch += reduce_scratch(k, w, *ends[i])
    part, coupling, update = pl.pallas_call(
        functools.partial(solve_kernel, inner, outer_, cols, split, 1.0 / (m * rows), widths, sliced),
        out_shape=(
            jax.ShapeDtypeStruct((k, share), f32),
            jax.ShapeDtypeStruct((k, width), f32),
            jax.ShapeDtypeStruct((k, width), bf16),
        ),
        in_specs=[hbm, hbm],
        out_specs=[hbm, hbm, hbm],
        scratch_shapes=scratch,
        compiler_params=pltpu.CompilerParams(collective_id=0, has_side_effects=True, vmem_limit_bytes=20 << 20),
        cost_estimate=pl.CostEstimate(flops=2 * m * k * (k + width), bytes_accessed=2 * m * (k + width), transcendentals=0),
        name="solve",
    )(panel, slab)
    if not sliced:
        part = lax.dynamic_slice_in_dim(part, lax.axis_index("col") * (k // cols), k // cols, 1)
    return part, coupling, update


def finish_kernel(chunks, part, coupling, update, panel, slab, part_out, coupling_out, out, kept, sems):
    copies = [
        pltpu.make_async_copy(coupling, coupling_out, sems.at[0]),
        pltpu.make_async_copy(part, part_out, sems.at[1]),
    ]
    for copy in copies:
        copy.start()
    rows = panel.shape[0] // chunks
    z = update[...]
    for t in range(chunks):
        at = pl.ds(t * rows, rows)
        taken = jnp.dot(panel[at, :], z, preferred_element_type=jnp.float32)
        kept[at, :] = (slab[at, :].astype(jnp.float32) - taken).astype(jnp.bfloat16)
        copies.append(pltpu.make_async_copy(kept.at[at], out.at[at], sems.at[2 + t]))
        copies[-1].start()
    for copy in copies:
        copy.wait()


def finish(part, coupling, update, panel, slab):
    m, k = panel.shape
    width = slab.shape[1]
    chunks = 8
    return pl.pallas_call(
        functools.partial(finish_kernel, chunks),
        out_shape=(
            jax.ShapeDtypeStruct(part.shape, part.dtype),
            jax.ShapeDtypeStruct(coupling.shape, coupling.dtype),
            jax.ShapeDtypeStruct((m, width), jnp.bfloat16),
        ),
        in_specs=[pl.BlockSpec(memory_space=pltpu.VMEM)] * 5,
        out_specs=[pl.BlockSpec(memory_space=pl.ANY)] * 3,
        scratch_shapes=[pltpu.VMEM((m, width), jnp.bfloat16), pltpu.SemaphoreType.DMA((2 + chunks,))],
        compiler_params=pltpu.CompilerParams(vmem_limit_bytes=12 << 20),
        cost_estimate=pl.CostEstimate(flops=2 * m * k * width, bytes_accessed=2 * m * (k + 2 * width), transcendentals=0),
        name="finish",
    )(part, coupling, update, panel, slab)


def on_device(panel, slab):
    rows, cols = lax.axis_size("row"), lax.axis_size("col")
    there = [pltpu.with_memory_space_constraint(x, pltpu.HBM) for x in (panel, slab)]
    part, coupling, update = solve(*there, rows, cols)
    return finish(part, coupling, update, panel, slab)


def solution(mesh):
    from jax.sharding import PartitionSpec as P

    return jax.shard_map(
        on_device,
        mesh=mesh,
        in_specs=(P("row", None), P("row", "col")),
        out_specs=(P(None, "col"), P(None, "col"), P("row", "col")),
        check_vma=False,
    )
```

```python
import functools

import jax
import jax.numpy as jnp
from jax import lax
from jax.experimental import pallas as pl
from jax.experimental.pallas import tpu as pltpu

HI = lax.Precision.HIGHEST
MESH = pl.DeviceIdType.MESH


def mm(a, b, ca=1, cb=0):
    return lax.dot_general(a, b, (((ca,), (cb,)), ((), ())), precision=HI, preferred_element_type=jnp.float32)


def row_of(x, s):
    return jnp.broadcast_to(x[s : s + 1, :], x.shape)


def lane_of(x, i):
    return jnp.broadcast_to(x[:, i : i + 1], x.shape)


def split3(x):
    hi = x.astype(jnp.bfloat16)
    rest = x - hi.astype(jnp.float32)
    mid = rest.astype(jnp.bfloat16)
    low = (rest - mid.astype(jnp.float32)).astype(jnp.bfloat16)
    return hi, mid, low


def outer(a, b):
    ah, am, al = split3(a)
    bh, bm, bl = split3(b)
    left = jnp.concatenate([ah, ah, am, ah, al, am], axis=0)
    right = jnp.concatenate([bh, bm, bh, bl, bh, bm], axis=0)
    return lax.dot_general(left, right, (((0,), (0,)), ((), ())), preferred_element_type=jnp.float32)


BLOCK, STEP, TILE = 32, 16, 128
PANEL_STEPS, SLAB_STEPS = 2, 2


def eliminate(m_ref, r_ref, w_ref, b):
    n = m_ref.shape[1]
    groups = BLOCK // 8
    shape = (8, TILE)
    sub = lax.broadcasted_iota(jnp.int32, shape, 0)
    lane = lax.broadcasted_iota(jnp.int32, shape, 1)
    top = b * BLOCK
    t, lo = top // TILE, top % TILE
    tiles = n // TILE
    inside = (lane >= lo) & (lane < lo + BLOCK)

    def rows(u):
        return [m_ref[top + 8 * g : top + 8 * g + 8, u * TILE : (u + 1) * TILE] for g in range(groups)]

    own = rows(t)
    unit = [jnp.where(inside, jnp.where(lane == sub + (lo + 8 * g), 1.0, 0.0), own[g]) for g in range(groups)]
    other = {u: rows(u) for u in range(tiles) if u != t}
    slabs = [own, unit] + list(other.values())
    for first in range(0, BLOCK, STEP):
        c = [{g: lane_of(own[g], lo + first + k) for g in range((first + k) // 8, groups)} for k in range(STEP)]
        for k in range(STEP):
            gj, sj = divmod(first + k, 8)
            inv = lax.rsqrt(row_of(c[k][gj], sj))
            l = {g: c[k][g] * inv for g in range(gj, groups)}
            for k2 in range(k + 1, STEP):
                g2, s2 = divmod(first + k2, 8)
                at = row_of(l[g2], s2)
                for g in range(g2, groups):
                    c[k2][g] = c[k2][g] - l[g] * at
            below = jnp.where(sub > sj, l[gj], 0.0)
            for x in slabs:
                pivot = row_of(x[gj], sj) * inv
                x[gj] = jnp.where(sub == sj, pivot, x[gj] - below * pivot)
                for g in range(gj + 1, groups):
                    x[g] = x[g] - l[g] * pivot
    zero = jnp.zeros(shape, jnp.float32)
    for g in range(groups):
        at = pl.ds(top + 8 * g, 8)
        for u in range(tiles):
            cols = pl.ds(u * TILE, TILE)
            if u == t:
                r_ref[at, cols] = jnp.where(lane >= sub + (lo + 8 * g), own[g], 0.0)
                w_ref[at, cols] = jnp.where(lane < lo + BLOCK, unit[g], 0.0)
            else:
                r_ref[at, cols] = other[u][g] if u > t else zero
                w_ref[at, cols] = other[u][g] if u < t else zero
    end = top + BLOCK
    if end < n:
        done = jnp.concatenate(
            [jnp.concatenate([unit[g] if u == t else other[u][g] for u in range(tiles)], axis=1) for g in range(groups)], axis=0
        )
        skip = (end // TILE) * TILE
        taken = outer(done[:, skip:], done)
        for u in range(tiles):
            cols = slice(u * TILE, (u + 1) * TILE)
            old = m_ref[end:, cols]
            if u == t:
                wide = lax.broadcasted_iota(jnp.int32, old.shape, 1)
                old = jnp.where((wide >= lo) & (wide < lo + BLOCK), 0.0, old)
            m_ref[end:, cols] = old - taken[end - skip :, cols]


def levels(rows):
    inner = 1
    while inner * inner * 4 <= rows:
        inner *= 2
    return inner, rows // inner


def send(src, dst, sems, index, to_row, to_col):
    copy = pltpu.make_async_remote_copy(
        src_ref=src, dst_ref=dst, send_sem=sems.at[0, index], recv_sem=sems.at[1, index],
        device_id={"row": to_row, "col": to_col}, device_id_type=MESH,
    )
    copy.start()
    return copy


def reduce_all(own, first_in, mid, second_in, result, sems, first, second, col):
    (na, ia, pa), (nb, ib, pb) = first, second
    ra = own.shape[0] // na
    rb = ra // nb
    used = 0

    def to(d, level, src, dst):
        nonlocal used
        used += 1
        return send(src, dst, sems, used - 1, level(d), col)

    sent = []
    for d in range(1, na):
        at = pl.multiple_of(((ia + d) % na) * ra, 8)
        sent.append(to(d, pa, own.at[pl.ds(at, ra)], first_in.at[d - 1]))
    yield
    here = pl.multiple_of(ia * ra, 8)
    total = own[pl.ds(here, ra), :]
    for d in range(1, na):
        sent[d - 1].wait()
        total = total + first_in[d - 1]
    sent = []
    if second_in.shape[0] < nb:
        mid[...] = total
        for d in range(1, nb):
            at = pl.multiple_of(((ib + d) % nb) * rb, 8)
            sent.append(to(d, pb, mid.at[pl.ds(at, rb)], second_in.at[d - 1]))
        yield
        total = mid[pl.ds(pl.multiple_of(ib * rb, 8), rb), :]
        for d in range(1, nb):
            sent[d - 1].wait()
            total = total + second_in[d - 1]
        spot = pl.multiple_of(ia * ra + ib * rb, 8)
        result[pl.ds(spot, rb), :] = total
        sent = []
        for d in range(1, nb):
            part = result.at[pl.ds(spot, rb)]
            sent.append(to(d, pb, part, part))
        yield
        for copy in sent:
            copy.wait()
    else:
        second_in[ib] = total
        for d in range(1, nb):
            sent.append(to(d, pb, second_in.at[ib], second_in.at[ib]))
        yield
        for copy in sent:
            copy.wait()
        total = second_in[0]
        for q in range(1, nb):
            total = total + second_in[q]
        result[pl.ds(here, ra), :] = total
    sent = []
    for d in range(1, na):
        part = result.at[pl.ds(here, ra)]
        sent.append(to(d, pa, part, part))
    yield
    for copy in sent:
        copy.wait()
    yield


def reduce_scratch(k, width, na, nb):
    f32 = jnp.float32
    ra = k // na
    rb = ra // nb
    second_in = (max(nb - 1, 1), rb, width) if rb % 8 == 0 else (nb, ra, width)
    return [
        pltpu.VMEM((k, width), f32),
        pltpu.VMEM((max(na - 1, 1), ra, width), f32),
        pltpu.VMEM((ra, width), f32),
        pltpu.VMEM(second_in, f32),
        pltpu.VMEM((k, width), f32),
        pltpu.SemaphoreType.DMA((2, 2 * (na - 1) + 2 * (nb - 1))),
    ]


def stacked(x, axis):
    h, m, l = split3(x)
    return jnp.concatenate([h, m, h, l, h, m] if axis is None else [h, h, m, h, l, m], axis=axis or 0)


def product(left, x, ca):
    return lax.dot_general(left, stacked(x, None), (((ca,), (0,)), ((), ())), preferred_element_type=jnp.float32)


PLAN = {'start': (0, 1, 2, 3), 'gram sent': (0, 1), 'gram last': (2, 3, 0, 1), 1: (2, 3), 2: (0, 1), 5: (2, 3)}
FAR_FIRST = ()


def solve_kernel(
    inner, outer_, cols, split, scale, halves, count, sliced,
    panel_hbm, slab_hbm, part, coupling, update, panel, slab,
    g_own, g_in, g_mid, g_all, m_ref, r_ref, w_ref, panel_sem, slab_sem, g_sem, *cross_refs,
):
    row = lax.axis_index("row")
    col = lax.axis_index("col")
    high, low = row // inner, row % inner
    f32 = jnp.float32
    all_cols = range(cols if split > 1 else 1)

    def near(d):
        return high * inner + (low + d) % inner

    def far(d):
        return ((high + d) % outer_) * inner + low

    def pieces(src, dst, sems):
        rows = src.shape[0] // sems.shape[0]
        parts = [pl.ds(t * rows, rows) for t in range(sems.shape[0])]
        return [pltpu.make_async_copy(src.at[at], dst.at[at], sems.at[t]) for t, at in enumerate(parts)]

    panel_loads = pieces(panel_hbm, panel, panel_sem)
    slab_loads = pieces(slab_hbm, slab, slab_sem)
    for copy in panel_loads:
        copy.start()

    barrier = pltpu.get_barrier_semaphore()
    greeted = 0
    for d in range(inner):
        for e in all_cols:
            if d or e:
                pl.semaphore_signal(barrier, 1, device_id={"row": near(d), "col": (col + e) % cols}, device_id_type=MESH)
                greeted += 1
    for d in range(1, outer_):
        pl.semaphore_signal(barrier, 1, device_id={"row": far(d), "col": col}, device_id_type=MESH)
        greeted += 1

    def tdot(a, b):
        return lax.dot_general(a, b, (((0,), (0,)), ((), ())), preferred_element_type=f32)

    h = g_own.shape[1]
    chunk = panel.shape[0] // len(panel_loads)
    for t, load in enumerate(panel_loads):
        load.wait()
        if t < len(slab_loads):
            slab_loads[t].start()
        p = panel[t * chunk : (t + 1) * chunk, :]
        top, low_right = tdot(p[:, :h], p), tdot(p[:, h:], p[:, h:])
        acc = (top, low_right) if t == 0 else (acc[0] + top, acc[1] + low_right)
    for copy in slab_loads[len(panel_loads) :]:
        copy.start()
    g_own[:h, :] = acc[0][:, :h] * scale
    g_own[h : 2 * h, :] = acc[0][:, h:] * scale
    g_own[2 * h :, :] = acc[1] * scale

    pl.semaphore_wait(barrier, greeted)

    share = g_own.shape[0] // split
    piece = share // inner
    base = (col * share) if split > 1 else 0
    sent = []
    for d in range(1, inner):
        at = pl.multiple_of(base + ((low + d) % inner) * piece, 8)
        sent.append(send(g_own.at[pl.ds(at, piece)], g_in.at[d - 1], g_sem, d - 1, near(d), col))
    used = inner - 1

    chunk = slab.shape[0] // len(slab_loads)
    for t, load in enumerate(slab_loads):
        load.wait()
        at = slice(t * chunk, (t + 1) * chunk)
        term = tdot(panel[at, :], slab[at, :])
        acc = term if t == 0 else acc + term
    acc = acc * scale
    ends = ((inner, low, near), (outer_, high, far))
    flows = []
    width = slab.shape[1] // count
    for i in range(count):
        refs = cross_refs[6 * i : 6 * i + 6]
        refs[0][...] = acc[:, i * width : (i + 1) * width]
        order = ends[::-1] if i in FAR_FIRST else ends
        flows.append(reduce_all(*refs, *order, col))

    def advance(point):
        for i in PLAN.get(point, ()):
            if i < count:
                next(flows[i])

    advance("start")

    mine = pl.multiple_of(base + low * piece, 8)
    total = g_own[pl.ds(mine, piece), :]
    for d in range(1, inner):
        sent[d - 1].wait()
        total = total + g_in[d - 1]
    g_mid[high] = total
    sent = []
    for d in range(1, outer_):
        sent.append(send(g_mid.at[high], g_mid.at[high], g_sem, used, far(d), col))
        used += 1
    advance("gram sent")
    for copy in sent:
        copy.wait()
    total = g_mid[0]
    for q in range(1, outer_):
        total = total + g_mid[q]
    g_all[pl.ds(mine, piece), :] = total
    sent = []
    for d in range(inner):
        for e in all_cols:
            if d or e:
                at = g_all.at[pl.ds(mine, piece)]
                sent.append(send(at, at, g_sem, used, near(d), (col + e) % cols))
                used += 1
    advance("gram back")
    advance("gram last")
    for copy in sent:
        copy.wait()

    m_ref[:h, :h] = g_all[:h, :]
    m_ref[:h, h:] = g_all[h : 2 * h, :]
    m_ref[h:, h:] = g_all[2 * h :, :]
    m_ref[h:, :h] = jnp.zeros((h, h), f32)
    for b in range(m_ref.shape[0] // BLOCK):
        eliminate(m_ref, r_ref, w_ref, b)
        advance(b)
    share = part.shape[1]
    if sliced:
        part[...] = r_ref[:, pl.ds(pl.multiple_of(col * share, TILE), share)]
    else:
        part[...] = r_ref[...]

    w = w_ref[...]
    across, down = stacked(w, 1), stacked(w, 0)
    each = count // halves
    half = slab.shape[1] // halves
    for t in range(halves):
        at = slice(t * half, (t + 1) * half)
        for flow in flows[t * each : (t + 1) * each]:
            for _ in flow:
                pass
        cross = jnp.concatenate([cross_refs[6 * i + 4][...] for i in range(t * each, (t + 1) * each)], axis=1)
        x = product(across, cross, 1)
        coupling[:, at] = x
        update[:, at] = product(down, x, 0).astype(jnp.bfloat16)


def solve(panel, slab, rows, cols):
    m, k = panel.shape
    width = slab.shape[1]
    inner, outer_ = levels(rows)
    h = k // 2
    split = cols if (3 * h) % (8 * inner * cols) == 0 else 1
    piece = 3 * h // split // inner
    sliced = (k // cols) % TILE == 0
    share = k // cols if sliced else k
    f32, bf16 = jnp.float32, jnp.bfloat16
    halves = 2 if width % (4 * TILE) == 0 else 1
    count = 4 if halves == 2 and k % (8 * rows) == 0 else halves
    g_copies = (inner - 1) + (outer_ - 1) + inner * (cols if split > 1 else 1) - 1
    hbm = pl.BlockSpec(memory_space=pl.ANY)
    scratch = [
        pltpu.VMEM((3 * h, h), f32),
        pltpu.VMEM((max(inner - 1, 1), piece, h), f32),
        pltpu.VMEM((outer_, piece, h), f32),
        pltpu.VMEM((3 * h, h), f32),
        pltpu.VMEM((k, k), f32),
        pltpu.VMEM((k, k), f32),
        pltpu.VMEM((k, k), f32),
        pltpu.SemaphoreType.DMA((PANEL_STEPS,)),
        pltpu.SemaphoreType.DMA((SLAB_STEPS,)),
        pltpu.SemaphoreType.DMA((2, g_copies)),
    ]
    for i in range(count):
        scratch += reduce_scratch(k, width // count, *((outer_, inner) if i in FAR_FIRST else (inner, outer_)))
    part, coupling, update, panel, slab = pl.pallas_call(
        functools.partial(solve_kernel, inner, outer_, cols, split, 1.0 / (m * rows), halves, count, sliced),
        out_shape=(
            jax.ShapeDtypeStruct((k, share), f32),
            jax.ShapeDtypeStruct((k, width), f32),
            jax.ShapeDtypeStruct((k, width), bf16),
            jax.ShapeDtypeStruct((m, k), bf16),
            jax.ShapeDtypeStruct((m, width), bf16),
        ),
        in_specs=[hbm, hbm],
        out_specs=[pl.BlockSpec(memory_space=pltpu.VMEM)] * 5,
        scratch_shapes=scratch,
        compiler_params=pltpu.CompilerParams(collective_id=0, has_side_effects=True, vmem_limit_bytes=20 << 20),
        cost_estimate=pl.CostEstimate(flops=2 * m * k * (k + width), bytes_accessed=2 * m * (k + width), transcendentals=0),
        name="solve",
    )(panel, slab)
    if not sliced:
        part = lax.dynamic_slice_in_dim(part, lax.axis_index("col") * (k // cols), k // cols, 1)
    return part, coupling, update, panel, slab


def finish_kernel(chunks, part, coupling, update, panel, slab, part_out, coupling_out, out, kept, sems):
    copies = [
        pltpu.make_async_copy(coupling, coupling_out, sems.at[0]),
        pltpu.make_async_copy(part, part_out, sems.at[1]),
    ]
    for copy in copies:
        copy.start()
    rows = panel.shape[0] // chunks
    z = update[...]
    for t in range(chunks):
        at = pl.ds(t * rows, rows)
        taken = jnp.dot(panel[at, :], z, preferred_element_type=jnp.float32)
        kept[at, :] = (slab[at, :].astype(jnp.float32) - taken).astype(jnp.bfloat16)
        copies.append(pltpu.make_async_copy(kept.at[at], out.at[at], sems.at[2 + t]))
        copies[-1].start()
    for copy in copies:
        copy.wait()


def finish(part, coupling, update, panel, slab):
    m, k = panel.shape
    width = slab.shape[1]
    chunks = 8
    return pl.pallas_call(
        functools.partial(finish_kernel, chunks),
        out_shape=(
            jax.ShapeDtypeStruct(part.shape, part.dtype),
            jax.ShapeDtypeStruct(coupling.shape, coupling.dtype),
            jax.ShapeDtypeStruct((m, width), jnp.bfloat16),
        ),
        in_specs=[pl.BlockSpec(memory_space=pltpu.VMEM)] * 5,
        out_specs=[pl.BlockSpec(memory_space=pl.ANY)] * 3,
        scratch_shapes=[pltpu.VMEM((m, width), jnp.bfloat16), pltpu.SemaphoreType.DMA((2 + chunks,))],
        compiler_params=pltpu.CompilerParams(vmem_limit_bytes=12 << 20),
        cost_estimate=pl.CostEstimate(flops=2 * m * k * width, bytes_accessed=2 * m * (k + 2 * width), transcendentals=0),
        name="finish",
    )(part, coupling, update, panel, slab)


def on_device(panel, slab):
    rows, cols = lax.axis_size("row"), lax.axis_size("col")
    there = [pltpu.with_memory_space_constraint(x, pltpu.HBM) for x in (panel, slab)]
    part, coupling, update, panel, slab = solve(*there, rows, cols)
    return finish(part, coupling, update, panel, slab)


def solution(mesh):
    from jax.sharding import PartitionSpec as P

    return jax.shard_map(
        on_device,
        mesh=mesh,
        in_specs=(P("row", None), P("row", "col")),
        out_specs=(P(None, "col"), P(None, "col"), P("row", "col")),
        check_vma=False,
    )
```

```python
import functools

import jax
import jax.numpy as jnp
from jax import lax
from jax.experimental import pallas as pl
from jax.experimental.pallas import tpu as pltpu

HI = lax.Precision.HIGHEST
MESH = pl.DeviceIdType.MESH


def mm(a, b, ca=1, cb=0):
    return lax.dot_general(a, b, (((ca,), (cb,)), ((), ())), precision=HI, preferred_element_type=jnp.float32)


def row_of(x, s):
    return jnp.broadcast_to(x[s : s + 1, :], x.shape)


def lane_of(x, i):
    return jnp.broadcast_to(x[:, i : i + 1], x.shape)


def split3(x):
    hi = x.astype(jnp.bfloat16)
    rest = x - hi.astype(jnp.float32)
    mid = rest.astype(jnp.bfloat16)
    low = (rest - mid.astype(jnp.float32)).astype(jnp.bfloat16)
    return hi, mid, low


def outer(a, b):
    ah, am, al = split3(a)
    bh, bm, bl = split3(b)
    left = jnp.concatenate([ah, ah, am, ah, al, am], axis=0)
    right = jnp.concatenate([bh, bm, bh, bl, bh, bm], axis=0)
    return lax.dot_general(left, right, (((0,), (0,)), ((), ())), preferred_element_type=jnp.float32)


BLOCK, STEP, TILE = 32, 16, 128
PANEL_STEPS = 2


def eliminate(m_ref, r_ref, w_ref, b):
    n = m_ref.shape[1]
    groups = BLOCK // 8
    shape = (8, TILE)
    sub = lax.broadcasted_iota(jnp.int32, shape, 0)
    lane = lax.broadcasted_iota(jnp.int32, shape, 1)
    top = b * BLOCK
    t, lo = top // TILE, top % TILE
    tiles = n // TILE
    inside = (lane >= lo) & (lane < lo + BLOCK)

    def rows(u):
        return [m_ref[top + 8 * g : top + 8 * g + 8, u * TILE : (u + 1) * TILE] for g in range(groups)]

    own = rows(t)
    unit = [jnp.where(inside, jnp.where(lane == sub + (lo + 8 * g), 1.0, 0.0), own[g]) for g in range(groups)]
    other = {u: rows(u) for u in range(tiles) if u != t}
    slabs = [own, unit] + list(other.values())
    for first in range(0, BLOCK, STEP):
        c = [{g: lane_of(own[g], lo + first + k) for g in range((first + k) // 8, groups)} for k in range(STEP)]
        for k in range(STEP):
            gj, sj = divmod(first + k, 8)
            inv = lax.rsqrt(row_of(c[k][gj], sj))
            l = {g: c[k][g] * inv for g in range(gj, groups)}
            for k2 in range(k + 1, STEP):
                g2, s2 = divmod(first + k2, 8)
                at = row_of(l[g2], s2)
                for g in range(g2, groups):
                    c[k2][g] = c[k2][g] - l[g] * at
            below = jnp.where(sub > sj, l[gj], 0.0)
            for x in slabs:
                pivot = row_of(x[gj], sj) * inv
                x[gj] = jnp.where(sub == sj, pivot, x[gj] - below * pivot)
                for g in range(gj + 1, groups):
                    x[g] = x[g] - l[g] * pivot
    zero = jnp.zeros(shape, jnp.float32)
    for g in range(groups):
        at = pl.ds(top + 8 * g, 8)
        for u in range(tiles):
            cols = pl.ds(u * TILE, TILE)
            if u == t:
                r_ref[at, cols] = jnp.where(lane >= sub + (lo + 8 * g), own[g], 0.0)
                w_ref[at, cols] = jnp.where(lane < lo + BLOCK, unit[g], 0.0)
            else:
                r_ref[at, cols] = other[u][g] if u > t else zero
                w_ref[at, cols] = other[u][g] if u < t else zero
    end = top + BLOCK
    if end < n:
        done = jnp.concatenate(
            [jnp.concatenate([unit[g] if u == t else other[u][g] for u in range(tiles)], axis=1) for g in range(groups)], axis=0
        )
        skip = (end // TILE) * TILE
        taken = outer(done[:, skip:], done)
        for u in range(tiles):
            cols = slice(u * TILE, (u + 1) * TILE)
            old = m_ref[end:, cols]
            if u == t:
                wide = lax.broadcasted_iota(jnp.int32, old.shape, 1)
                old = jnp.where((wide >= lo) & (wide < lo + BLOCK), 0.0, old)
            m_ref[end:, cols] = old - taken[end - skip :, cols]


def levels(rows):
    inner = 1
    while inner * inner * 4 <= rows:
        inner *= 2
    return inner, rows // inner


def send(src, dst, sems, index, to_row, to_col):
    copy = pltpu.make_async_remote_copy(
        src_ref=src, dst_ref=dst, send_sem=sems.at[0, index], recv_sem=sems.at[1, index],
        device_id={"row": to_row, "col": to_col}, device_id_type=MESH,
    )
    copy.start()
    return copy


def reduce_all(own, first_in, mid, second_in, result, sems, first, second, col):
    (na, ia, pa, qa), (nb, ib, pb, qb) = first, second
    ra = own.shape[0] // na
    rb = ra // nb
    used = 0

    def to(d, level, src, dst):
        nonlocal used
        used += 1
        return send(src, dst, sems, used - 1, level(d), col)

    sent = []
    for d in reversed(range(1, na)):
        at = pl.multiple_of(qa(d) * ra, 8)
        sent.append(to(d, pa, own.at[pl.ds(at, ra)], first_in.at[d - 1]))
    yield
    here = pl.multiple_of(ia * ra, 8)
    total = own[pl.ds(here, ra), :]
    for d in range(1, na):
        sent[-d].wait()
        total = total + first_in[d - 1]
    sent = []
    if second_in.shape[0] < nb:
        mid[...] = total
        for d in range(1, nb):
            at = pl.multiple_of(qb(d) * rb, 8)
            sent.append(to(d, pb, mid.at[pl.ds(at, rb)], second_in.at[d - 1]))
        yield
        total = mid[pl.ds(pl.multiple_of(ib * rb, 8), rb), :]
        for d in range(1, nb):
            sent[d - 1].wait()
            total = total + second_in[d - 1]
        spot = pl.multiple_of(ia * ra + ib * rb, 8)
        result[pl.ds(spot, rb), :] = total
        sent = []
        for d in range(1, nb):
            part = result.at[pl.ds(spot, rb)]
            sent.append(to(d, pb, part, part))
        yield
        for copy in sent:
            copy.wait()
    else:
        second_in[ib] = total
        for d in range(1, nb):
            sent.append(to(d, pb, second_in.at[ib], second_in.at[ib]))
        yield
        for copy in sent:
            copy.wait()
        total = second_in[0]
        for q in range(1, nb):
            total = total + second_in[q]
        result[pl.ds(here, ra), :] = total
    sent = []
    for d in reversed(range(1, na)):
        part = result.at[pl.ds(here, ra)]
        sent.append(to(d, pa, part, part))
    yield
    for copy in sent:
        copy.wait()
    yield


def reduce_scratch(k, width, na, nb):
    f32 = jnp.float32
    ra = k // na
    rb = ra // nb
    second_in = (max(nb - 1, 1), rb, width) if rb % 8 == 0 else (nb, ra, width)
    return [
        pltpu.VMEM((k, width), f32),
        pltpu.VMEM((max(na - 1, 1), ra, width), f32),
        pltpu.VMEM((ra, width), f32),
        pltpu.VMEM(second_in, f32),
        pltpu.VMEM((k, width), f32),
        pltpu.SemaphoreType.DMA((2, 2 * (na - 1) + 2 * (nb - 1))),
    ]


def stacked(x, axis):
    h, m, l = split3(x)
    return jnp.concatenate([h, h, m, h, l, m] if axis else [h, m, h, l, h, m], axis=axis)


def product(left, x):
    right = stacked(x, 0)
    mid = right.shape[0] // 2
    return jnp.dot(left[:, :mid], right[:mid, :], preferred_element_type=jnp.float32) + jnp.dot(
        left[:, mid:], right[mid:, :], preferred_element_type=jnp.float32
    )


PLAN = {('start', 0): (0, 1), ('start', 1): (2, 3), 'gram sent': (0, 1), 'gram last': (2, 3, 0, 1), 0: (2,), 1: (3, 0), 2: (1,), 4: (2, 3)}
FAR_FIRST = ()


def solve_kernel(
    inner, outer_, cols, split, scale, halves, count, sliced,
    panel_hbm, slab_hbm, part, coupling, update, panel, slab,
    g_own, g_in, g_mid, g_all, m_ref, r_ref, w_ref, panel_sem, slab_sem, g_sem, *cross_refs,
):
    row = lax.axis_index("row")
    col = lax.axis_index("col")
    high, low = row // inner, row % inner
    f32 = jnp.float32
    all_cols = range(cols if split > 1 else 1)

    def other(d):
        at = low
        bit = 1
        while bit < inner:
            if d & bit:
                at = at + bit * (1 - 2 * ((low // bit) % 2))
            bit *= 2
        return at

    def near(d):
        return high * inner + other(d)

    def far(d):
        return ((high + d) % outer_) * inner + low

    def pieces(src, dst, sems):
        rows = src.shape[0] // sems.shape[0]
        parts = [pl.ds(t * rows, rows) for t in range(sems.shape[0])]
        return [pltpu.make_async_copy(src.at[at], dst.at[at], sems.at[t]) for t, at in enumerate(parts)]

    panel_loads = pieces(panel_hbm, panel, panel_sem)
    half = slab.shape[1] // halves
    columns = [(slice(None), pl.ds(t * half, half)) for t in range(halves)]
    slab_loads = [pltpu.make_async_copy(slab_hbm.at[at], slab.at[at], slab_sem.at[t]) for t, at in enumerate(columns)]
    for copy in panel_loads:
        copy.start()

    barrier = pltpu.get_barrier_semaphore()
    greeted = 0
    for d in range(inner):
        for e in all_cols:
            if d or e:
                pl.semaphore_signal(barrier, 1, device_id={"row": near(d), "col": (col + e) % cols}, device_id_type=MESH)
                greeted += 1
    for d in range(1, outer_):
        pl.semaphore_signal(barrier, 1, device_id={"row": far(d), "col": col}, device_id_type=MESH)
        greeted += 1

    def tdot(a, b):
        return lax.dot_general(a, b, (((0,), (0,)), ((), ())), preferred_element_type=f32)

    h = g_own.shape[1]
    chunk = panel.shape[0] // len(panel_loads)
    for t, load in enumerate(panel_loads):
        load.wait()
        if t < len(slab_loads):
            slab_loads[t].start()
        p = panel[t * chunk : (t + 1) * chunk, :]
        top, low_right = tdot(p[:, :h], p), tdot(p[:, h:], p[:, h:])
        acc = (top, low_right) if t == 0 else (acc[0] + top, acc[1] + low_right)
    for copy in slab_loads[len(panel_loads) :]:
        copy.start()
    g_own[:h, :] = acc[0][:, :h] * scale
    g_own[h : 2 * h, :] = acc[0][:, h:] * scale
    g_own[2 * h :, :] = acc[1] * scale

    pl.semaphore_wait(barrier, greeted)

    share = g_own.shape[0] // split
    piece = share // inner
    base = (col * share) if split > 1 else 0
    sent = []
    for d in reversed(range(1, inner)):
        at = pl.multiple_of(base + other(d) * piece, 8)
        sent.append(send(g_own.at[pl.ds(at, piece)], g_in.at[d - 1], g_sem, d - 1, near(d), col))
    used = inner - 1

    ends = ((inner, low, near, other), (outer_, high, far, lambda d: (high + d) % outer_))
    flows = []
    each = count // halves
    width = half // each
    mid = panel.shape[0] // 2

    def advance(point):
        for i in PLAN.get(point, ()):
            if i < len(flows):
                next(flows[i])

    for t, load in enumerate(slab_loads):
        load.wait()
        at = slice(t * half, (t + 1) * half)
        acc = tdot(panel[:mid, :], slab[:mid, at]) + tdot(panel[mid:, :], slab[mid:, at])
        acc = acc * scale
        for i in range(each):
            refs = cross_refs[6 * len(flows) : 6 * len(flows) + 6]
            refs[0][...] = acc[:, i * width : (i + 1) * width]
            order = ends[::-1] if len(flows) in FAR_FIRST else ends
            flows.append(reduce_all(*refs, *order, col))
        advance(("start", t))

    mine = pl.multiple_of(base + low * piece, 8)
    total = g_own[pl.ds(mine, piece), :]
    for d in range(1, inner):
        sent[-d].wait()
        total = total + g_in[d - 1]
    g_mid[high] = total
    sent = []
    for d in range(1, outer_):
        sent.append(send(g_mid.at[high], g_mid.at[high], g_sem, used, far(d), col))
        used += 1
    advance("gram sent")
    for copy in sent:
        copy.wait()
    total = g_mid[0]
    for q in range(1, outer_):
        total = total + g_mid[q]
    g_all[pl.ds(mine, piece), :] = total
    sent = []
    for d in reversed(range(inner)):
        for e in all_cols:
            if d or e:
                at = g_all.at[pl.ds(mine, piece)]
                sent.append(send(at, at, g_sem, used, near(d), (col + e) % cols))
                used += 1
    advance("gram back")
    advance("gram last")
    for copy in sent:
        copy.wait()

    m_ref[:h, :h] = g_all[:h, :]
    m_ref[:h, h:] = g_all[h : 2 * h, :]
    m_ref[h:, h:] = g_all[2 * h :, :]
    m_ref[h:, :h] = jnp.zeros((h, h), f32)
    for b in range(m_ref.shape[0] // BLOCK):
        eliminate(m_ref, r_ref, w_ref, b)
        advance(b)
    share = part.shape[1]
    if sliced:
        part[...] = r_ref[:, pl.ds(pl.multiple_of(col * share, TILE), share)]
    else:
        part[...] = r_ref[...]

    w = w_ref[...]
    across, down = stacked(w, 1), stacked(w.T, 1)
    for t in range(halves):
        at = slice(t * half, (t + 1) * half)
        for flow in flows[t * each : (t + 1) * each]:
            for _ in flow:
                pass
        cross = jnp.concatenate([cross_refs[6 * i + 4][...] for i in range(t * each, (t + 1) * each)], axis=1)
        x = product(across, cross)
        coupling[:, at] = x
        update[:, at] = product(down, x).astype(jnp.bfloat16)


def solve(panel, slab, rows, cols):
    m, k = panel.shape
    width = slab.shape[1]
    inner, outer_ = levels(rows)
    h = k // 2
    split = cols if (3 * h) % (8 * inner * cols) == 0 else 1
    piece = 3 * h // split // inner
    sliced = (k // cols) % TILE == 0
    share = k // cols if sliced else k
    f32, bf16 = jnp.float32, jnp.bfloat16
    halves = 2 if width % (4 * TILE) == 0 else 1
    count = 4 if halves == 2 and k % (8 * rows) == 0 else halves
    g_copies = (inner - 1) + (outer_ - 1) + inner * (cols if split > 1 else 1) - 1
    hbm = pl.BlockSpec(memory_space=pl.ANY)
    scratch = [
        pltpu.VMEM((3 * h, h), f32),
        pltpu.VMEM((max(inner - 1, 1), piece, h), f32),
        pltpu.VMEM((outer_, piece, h), f32),
        pltpu.VMEM((3 * h, h), f32),
        pltpu.VMEM((k, k), f32),
        pltpu.VMEM((k, k), f32),
        pltpu.VMEM((k, k), f32),
        pltpu.SemaphoreType.DMA((PANEL_STEPS,)),
        pltpu.SemaphoreType.DMA((halves,)),
        pltpu.SemaphoreType.DMA((2, g_copies)),
    ]
    for i in range(count):
        scratch += reduce_scratch(k, width // count, *((outer_, inner) if i in FAR_FIRST else (inner, outer_)))
    part, coupling, update, panel, slab = pl.pallas_call(
        functools.partial(solve_kernel, inner, outer_, cols, split, 1.0 / (m * rows), halves, count, sliced),
        out_shape=(
            jax.ShapeDtypeStruct((k, share), f32),
            jax.ShapeDtypeStruct((k, width), f32),
            jax.ShapeDtypeStruct((k, width), bf16),
            jax.ShapeDtypeStruct((m, k), bf16),
            jax.ShapeDtypeStruct((m, width), bf16),
        ),
        in_specs=[hbm, hbm],
        out_specs=[pl.BlockSpec(memory_space=pltpu.VMEM)] * 5,
        scratch_shapes=scratch,
        compiler_params=pltpu.CompilerParams(collective_id=0, has_side_effects=True, vmem_limit_bytes=20 << 20),
        cost_estimate=pl.CostEstimate(flops=2 * m * k * (k + width), bytes_accessed=2 * m * (k + width), transcendentals=0),
        name="solve",
    )(panel, slab)
    if not sliced:
        part = lax.dynamic_slice_in_dim(part, lax.axis_index("col") * (k // cols), k // cols, 1)
    return part, coupling, update, panel, slab


def finish_kernel(chunks, part, coupling, update, panel, slab, part_out, coupling_out, out, kept, sems):
    copies = [
        pltpu.make_async_copy(coupling, coupling_out, sems.at[0]),
        pltpu.make_async_copy(part, part_out, sems.at[1]),
    ]
    for copy in copies:
        copy.start()
    rows = panel.shape[0] // chunks
    z = update[...]
    for t in range(chunks):
        at = pl.ds(t * rows, rows)
        taken = jnp.dot(panel[at, :], z, preferred_element_type=jnp.float32)
        kept[at, :] = (slab[at, :].astype(jnp.float32) - taken).astype(jnp.bfloat16)
        copies.append(pltpu.make_async_copy(kept.at[at], out.at[at], sems.at[2 + t]))
        copies[-1].start()
    for copy in copies:
        copy.wait()


def finish(part, coupling, update, panel, slab):
    m, k = panel.shape
    width = slab.shape[1]
    chunks = 8
    return pl.pallas_call(
        functools.partial(finish_kernel, chunks),
        out_shape=(
            jax.ShapeDtypeStruct(part.shape, part.dtype),
            jax.ShapeDtypeStruct(coupling.shape, coupling.dtype),
            jax.ShapeDtypeStruct((m, width), jnp.bfloat16),
        ),
        in_specs=[pl.BlockSpec(memory_space=pltpu.VMEM)] * 5,
        out_specs=[pl.BlockSpec(memory_space=pl.ANY)] * 3,
        scratch_shapes=[pltpu.VMEM((m, width), jnp.bfloat16), pltpu.SemaphoreType.DMA((2 + chunks,))],
        compiler_params=pltpu.CompilerParams(vmem_limit_bytes=12 << 20),
        cost_estimate=pl.CostEstimate(flops=2 * m * k * width, bytes_accessed=2 * m * (k + 2 * width), transcendentals=0),
        name="finish",
    )(part, coupling, update, panel, slab)


def on_device(panel, slab):
    rows, cols = lax.axis_size("row"), lax.axis_size("col")
    there = [pltpu.with_memory_space_constraint(x, pltpu.HBM) for x in (panel, slab)]
    part, coupling, update, panel, slab = solve(*there, rows, cols)
    return finish(part, coupling, update, panel, slab)


def solution(mesh):
    from jax.sharding import PartitionSpec as P

    return jax.shard_map(
        on_device,
        mesh=mesh,
        in_specs=(P("row", None), P("row", "col")),
        out_specs=(P(None, "col"), P(None, "col"), P("row", "col")),
        check_vma=False,
    )
```

```python
import functools

import jax
import jax.numpy as jnp
from jax import lax
from jax.experimental import pallas as pl
from jax.experimental.pallas import tpu as pltpu

HI = lax.Precision.HIGHEST
MESH = pl.DeviceIdType.MESH


def mm(a, b, ca=1, cb=0):
    return lax.dot_general(a, b, (((ca,), (cb,)), ((), ())), precision=HI, preferred_element_type=jnp.float32)


def row_of(x, s):
    return jnp.broadcast_to(x[s : s + 1, :], x.shape)


def lane_of(x, i):
    return jnp.broadcast_to(x[:, i : i + 1], x.shape)


def split3(x):
    hi = x.astype(jnp.bfloat16)
    rest = x - hi.astype(jnp.float32)
    mid = rest.astype(jnp.bfloat16)
    low = (rest - mid.astype(jnp.float32)).astype(jnp.bfloat16)
    return hi, mid, low


def outer(a, b):
    ah, am, al = split3(a)
    bh, bm, bl = split3(b)
    left = jnp.concatenate([ah, ah, am, ah, al, am], axis=0)
    right = jnp.concatenate([bh, bm, bh, bl, bh, bm], axis=0)
    return lax.dot_general(left, right, (((0,), (0,)), ((), ())), preferred_element_type=jnp.float32)


BLOCK, STEP, TILE = 32, 16, 128
PANEL_STEPS = 4


def eliminate(m_ref, r_ref, w_ref, b):
    n = m_ref.shape[1]
    groups = BLOCK // 8
    shape = (8, TILE)
    sub = lax.broadcasted_iota(jnp.int32, shape, 0)
    lane = lax.broadcasted_iota(jnp.int32, shape, 1)
    top = b * BLOCK
    t, lo = top // TILE, top % TILE
    tiles = n // TILE
    inside = (lane >= lo) & (lane < lo + BLOCK)

    def rows(u):
        return [m_ref[top + 8 * g : top + 8 * g + 8, u * TILE : (u + 1) * TILE] for g in range(groups)]

    own = rows(t)
    unit = [jnp.where(inside, jnp.where(lane == sub + (lo + 8 * g), 1.0, 0.0), own[g]) for g in range(groups)]
    other = {u: rows(u) for u in range(tiles) if u != t}
    slabs = [own, unit] + list(other.values())
    for first in range(0, BLOCK, STEP):
        c = [{g: lane_of(own[g], lo + first + k) for g in range((first + k) // 8, groups)} for k in range(STEP)]
        for k in range(STEP):
            gj, sj = divmod(first + k, 8)
            inv = lax.rsqrt(row_of(c[k][gj], sj))
            l = {g: c[k][g] * inv for g in range(gj, groups)}
            for k2 in range(k + 1, STEP):
                g2, s2 = divmod(first + k2, 8)
                at = row_of(l[g2], s2)
                for g in range(g2, groups):
                    c[k2][g] = c[k2][g] - l[g] * at
            below = jnp.where(sub > sj, l[gj], 0.0)
            for x in slabs:
                pivot = row_of(x[gj], sj) * inv
                x[gj] = jnp.where(sub == sj, pivot, x[gj] - below * pivot)
                for g in range(gj + 1, groups):
                    x[g] = x[g] - l[g] * pivot
    zero = jnp.zeros(shape, jnp.float32)
    for g in range(groups):
        at = pl.ds(top + 8 * g, 8)
        for u in range(tiles):
            cols = pl.ds(u * TILE, TILE)
            if u == t:
                r_ref[at, cols] = jnp.where(lane >= sub + (lo + 8 * g), own[g], 0.0)
                w_ref[at, cols] = jnp.where(lane < lo + BLOCK, unit[g], 0.0)
            else:
                r_ref[at, cols] = other[u][g] if u > t else zero
                w_ref[at, cols] = other[u][g] if u < t else zero
    end = top + BLOCK
    if end < n:
        done = jnp.concatenate(
            [jnp.concatenate([unit[g] if u == t else other[u][g] for u in range(tiles)], axis=1) for g in range(groups)], axis=0
        )
        skip = (end // TILE) * TILE
        taken = outer(done[:, skip:], done)
        for u in range(tiles):
            cols = slice(u * TILE, (u + 1) * TILE)
            old = m_ref[end:, cols]
            if u == t:
                wide = lax.broadcasted_iota(jnp.int32, old.shape, 1)
                old = jnp.where((wide >= lo) & (wide < lo + BLOCK), 0.0, old)
            m_ref[end:, cols] = old - taken[end - skip :, cols]


def levels(rows):
    inner = 1
    while inner * inner * 4 <= rows:
        inner *= 2
    return inner, rows // inner


def send(src, dst, sems, index, to_row, to_col):
    copy = pltpu.make_async_remote_copy(
        src_ref=src, dst_ref=dst, send_sem=sems.at[0, index], recv_sem=sems.at[1, index],
        device_id={"row": to_row, "col": to_col}, device_id_type=MESH,
    )
    copy.start()
    return copy


def reduce_all(own, first_in, mid, second_in, result, sems, first, second, col):
    (na, ia, pa, qa), (nb, ib, pb, qb) = first, second
    ra = own.shape[0] // na
    rb = ra // nb
    used = 0

    def to(d, level, src, dst):
        nonlocal used
        used += 1
        return send(src, dst, sems, used - 1, level(d), col)

    sent = []
    for d in reversed(range(1, na)):
        at = pl.multiple_of(qa(d) * ra, 8)
        sent.append(to(d, pa, own.at[pl.ds(at, ra)], first_in.at[d - 1]))
    yield
    here = pl.multiple_of(ia * ra, 8)
    total = own[pl.ds(here, ra), :]
    for d in range(1, na):
        sent[-d].wait()
        total = total + first_in[d - 1]
    sent = []
    if second_in.shape[0] < nb:
        mid[...] = total
        for d in range(1, nb):
            at = pl.multiple_of(qb(d) * rb, 8)
            sent.append(to(d, pb, mid.at[pl.ds(at, rb)], second_in.at[d - 1]))
        yield
        total = mid[pl.ds(pl.multiple_of(ib * rb, 8), rb), :]
        for d in range(1, nb):
            sent[d - 1].wait()
            total = total + second_in[d - 1]
        spot = pl.multiple_of(ia * ra + ib * rb, 8)
        result[pl.ds(spot, rb), :] = total
        sent = []
        for d in range(1, nb):
            part = result.at[pl.ds(spot, rb)]
            sent.append(to(d, pb, part, part))
        yield
        for copy in sent:
            copy.wait()
    else:
        second_in[ib] = total
        for d in range(1, nb):
            sent.append(to(d, pb, second_in.at[ib], second_in.at[ib]))
        yield
        for copy in sent:
            copy.wait()
        total = second_in[0]
        for q in range(1, nb):
            total = total + second_in[q]
        result[pl.ds(here, ra), :] = total
    sent = []
    for d in reversed(range(1, na)):
        part = result.at[pl.ds(here, ra)]
        sent.append(to(d, pa, part, part))
    yield
    for copy in sent:
        copy.wait()
    yield


def reduce_scratch(k, width, na, nb):
    f32 = jnp.float32
    ra = k // na
    rb = ra // nb
    second_in = (max(nb - 1, 1), rb, width) if rb % 8 == 0 else (nb, ra, width)
    return [
        pltpu.VMEM((k, width), f32),
        pltpu.VMEM((max(na - 1, 1), ra, width), f32),
        pltpu.VMEM((ra, width), f32),
        pltpu.VMEM(second_in, f32),
        pltpu.VMEM((k, width), f32),
        pltpu.SemaphoreType.DMA((2, 2 * (na - 1) + 2 * (nb - 1))),
    ]


def stacked(x, axis):
    h, m, l = split3(x)
    return jnp.concatenate([h, h, m, h, l, m] if axis else [h, m, h, l, h, m], axis=axis)


def product(left, x):
    right = stacked(x, 0)
    mid = right.shape[0] // 2
    return jnp.dot(left[:, :mid], right[:mid, :], preferred_element_type=jnp.float32) + jnp.dot(
        left[:, mid:], right[mid:, :], preferred_element_type=jnp.float32
    )


PLAN = {('start', 0): (0, 1), ('start', 1): (2, 3), 'gram sent': (0, 1), 'gram last': (2, 3, 0, 1), 0: (2,), 1: (0, 3, 1), 4: (2, 3)}
FAR_FIRST = ()


def solve_kernel(
    inner, outer_, cols, split, scale, halves, count, sliced,
    panel_hbm, slab_hbm, part, coupling, update, panel, slab,
    g_own, g_in, g_mid, g_all, m_ref, r_ref, w_ref, panel_sem, slab_sem, g_sem, *cross_refs,
):
    row = lax.axis_index("row")
    col = lax.axis_index("col")
    high, low = row // inner, row % inner
    f32 = jnp.float32
    all_cols = range(cols if split > 1 else 1)

    def other(d):
        at = low
        bit = 1
        while bit < inner:
            if d & bit:
                at = at + bit * (1 - 2 * ((low // bit) % 2))
            bit *= 2
        return at

    def near(d):
        return high * inner + other(d)

    def far(d):
        return ((high + d) % outer_) * inner + low

    def pieces(src, dst, sems):
        rows = src.shape[0] // sems.shape[0]
        parts = [pl.ds(t * rows, rows) for t in range(sems.shape[0])]
        return [pltpu.make_async_copy(src.at[at], dst.at[at], sems.at[t]) for t, at in enumerate(parts)]

    panel_loads = pieces(panel_hbm, panel, panel_sem)
    half = slab.shape[1] // halves
    columns = [(slice(None), pl.ds(t * half, half)) for t in range(halves)]
    slab_loads = [pltpu.make_async_copy(slab_hbm.at[at], slab.at[at], slab_sem.at[t]) for t, at in enumerate(columns)]
    for copy in panel_loads:
        copy.start()

    barrier = pltpu.get_barrier_semaphore()
    greeted = 0
    for d in range(inner):
        for e in all_cols:
            if d or e:
                pl.semaphore_signal(barrier, 1, device_id={"row": near(d), "col": (col + e) % cols}, device_id_type=MESH)
                greeted += 1
    for d in range(1, outer_):
        pl.semaphore_signal(barrier, 1, device_id={"row": far(d), "col": col}, device_id_type=MESH)
        greeted += 1

    def tdot(a, b):
        return lax.dot_general(a, b, (((0,), (0,)), ((), ())), preferred_element_type=f32)

    h = g_own.shape[1]
    chunk = panel.shape[0] // len(panel_loads)
    for t, load in enumerate(panel_loads):
        load.wait()
        if t < len(slab_loads):
            slab_loads[t].start()
        p = panel[t * chunk : (t + 1) * chunk, :]
        top, low_right = tdot(p[:, :h], p), tdot(p[:, h:], p[:, h:])
        acc = (top, low_right) if t == 0 else (acc[0] + top, acc[1] + low_right)
    for copy in slab_loads[len(panel_loads) :]:
        copy.start()
    g_own[:h, :] = acc[0][:, :h] * scale
    g_own[h : 2 * h, :] = acc[0][:, h:] * scale
    g_own[2 * h :, :] = acc[1] * scale

    pl.semaphore_wait(barrier, greeted)

    share = g_own.shape[0] // split
    piece = share // inner
    base = (col * share) if split > 1 else 0
    sent = []
    for d in reversed(range(1, inner)):
        at = pl.multiple_of(base + other(d) * piece, 8)
        sent.append(send(g_own.at[pl.ds(at, piece)], g_in.at[d - 1], g_sem, d - 1, near(d), col))
    used = inner - 1

    ends = ((inner, low, near, other), (outer_, high, far, lambda d: (high + d) % outer_))
    flows = []
    each = count // halves
    width = half // each
    mid = panel.shape[0] // 2

    def advance(point):
        for i in PLAN.get(point, ()):
            if i < len(flows):
                next(flows[i])

    for t, load in enumerate(slab_loads):
        load.wait()
        at = slice(t * half, (t + 1) * half)
        acc = tdot(panel[:mid, :], slab[:mid, at]) + tdot(panel[mid:, :], slab[mid:, at])
        acc = acc * scale
        for i in range(each):
            refs = cross_refs[6 * len(flows) : 6 * len(flows) + 6]
            refs[0][...] = acc[:, i * width : (i + 1) * width]
            order = ends[::-1] if len(flows) in FAR_FIRST else ends
            flows.append(reduce_all(*refs, *order, col))
        advance(("start", t))

    mine = pl.multiple_of(base + low * piece, 8)
    total = g_own[pl.ds(mine, piece), :]
    for d in range(1, inner):
        sent[-d].wait()
        total = total + g_in[d - 1]
    g_mid[high] = total
    sent = []
    for d in range(1, outer_):
        sent.append(send(g_mid.at[high], g_mid.at[high], g_sem, used, far(d), col))
        used += 1
    advance("gram sent")
    for copy in sent:
        copy.wait()
    total = g_mid[0]
    for q in range(1, outer_):
        total = total + g_mid[q]
    g_all[pl.ds(mine, piece), :] = total
    sent = []
    for d in reversed(range(inner)):
        for e in all_cols:
            if d or e:
                at = g_all.at[pl.ds(mine, piece)]
                sent.append(send(at, at, g_sem, used, near(d), (col + e) % cols))
                used += 1
    advance("gram back")
    advance("gram last")
    for copy in sent:
        copy.wait()

    m_ref[:h, :h] = g_all[:h, :]
    m_ref[:h, h:] = g_all[h : 2 * h, :]
    m_ref[h:, h:] = g_all[2 * h :, :]
    m_ref[h:, :h] = jnp.zeros((h, h), f32)
    for b in range(m_ref.shape[0] // BLOCK):
        eliminate(m_ref, r_ref, w_ref, b)
        advance(b)
    share = part.shape[1]
    if sliced:
        part[...] = r_ref[:, pl.ds(pl.multiple_of(col * share, TILE), share)]
    else:
        part[...] = r_ref[...]

    w = w_ref[...]
    left = jnp.concatenate([w, product(stacked(w.T, 1), w)], axis=0)
    left = stacked(left, 1)
    k = w.shape[0]
    for t in range(halves):
        at = slice(t * half, (t + 1) * half)
        for flow in flows[t * each : (t + 1) * each]:
            for _ in flow:
                pass
        cross = jnp.concatenate([cross_refs[6 * i + 4][...] for i in range(t * each, (t + 1) * each)], axis=1)
        x = product(left, cross)
        coupling[:, at] = x[:k, :]
        update[:, at] = x[k:, :].astype(jnp.bfloat16)


def solve(panel, slab, rows, cols):
    m, k = panel.shape
    width = slab.shape[1]
    inner, outer_ = levels(rows)
    h = k // 2
    split = cols if (3 * h) % (8 * inner * cols) == 0 else 1
    piece = 3 * h // split // inner
    sliced = (k // cols) % TILE == 0
    share = k // cols if sliced else k
    f32, bf16 = jnp.float32, jnp.bfloat16
    halves = 2 if width % (4 * TILE) == 0 else 1
    count = 4 if halves == 2 and k % (8 * rows) == 0 else halves
    g_copies = (inner - 1) + (outer_ - 1) + inner * (cols if split > 1 else 1) - 1
    hbm = pl.BlockSpec(memory_space=pl.ANY)
    scratch = [
        pltpu.VMEM((3 * h, h), f32),
        pltpu.VMEM((max(inner - 1, 1), piece, h), f32),
        pltpu.VMEM((outer_, piece, h), f32),
        pltpu.VMEM((3 * h, h), f32),
        pltpu.VMEM((k, k), f32),
        pltpu.VMEM((k, k), f32),
        pltpu.VMEM((k, k), f32),
        pltpu.SemaphoreType.DMA((PANEL_STEPS,)),
        pltpu.SemaphoreType.DMA((halves,)),
        pltpu.SemaphoreType.DMA((2, g_copies)),
    ]
    for i in range(count):
        scratch += reduce_scratch(k, width // count, *((outer_, inner) if i in FAR_FIRST else (inner, outer_)))
    part, coupling, update, panel, slab = pl.pallas_call(
        functools.partial(solve_kernel, inner, outer_, cols, split, 1.0 / (m * rows), halves, count, sliced),
        out_shape=(
            jax.ShapeDtypeStruct((k, share), f32),
            jax.ShapeDtypeStruct((k, width), f32),
            jax.ShapeDtypeStruct((k, width), bf16),
            jax.ShapeDtypeStruct((m, k), bf16),
            jax.ShapeDtypeStruct((m, width), bf16),
        ),
        in_specs=[hbm, hbm],
        out_specs=[pl.BlockSpec(memory_space=pltpu.VMEM)] * 5,
        scratch_shapes=scratch,
        compiler_params=pltpu.CompilerParams(collective_id=0, has_side_effects=True, vmem_limit_bytes=20 << 20),
        cost_estimate=pl.CostEstimate(flops=2 * m * k * (k + width), bytes_accessed=2 * m * (k + width), transcendentals=0),
        name="solve",
    )(panel, slab)
    if not sliced:
        part = lax.dynamic_slice_in_dim(part, lax.axis_index("col") * (k // cols), k // cols, 1)
    return part, coupling, update, panel, slab


def finish_kernel(chunks, part, coupling, update, panel, slab, part_out, coupling_out, out, kept, sems):
    copies = [
        pltpu.make_async_copy(coupling, coupling_out, sems.at[0]),
        pltpu.make_async_copy(part, part_out, sems.at[1]),
    ]
    for copy in copies:
        copy.start()
    rows = panel.shape[0] // chunks
    z = update[...]
    for t in range(chunks):
        at = pl.ds(t * rows, rows)
        taken = jnp.dot(panel[at, :], z, preferred_element_type=jnp.float32)
        kept[at, :] = (slab[at, :].astype(jnp.float32) - taken).astype(jnp.bfloat16)
        copies.append(pltpu.make_async_copy(kept.at[at], out.at[at], sems.at[2 + t]))
        copies[-1].start()
    for copy in copies:
        copy.wait()


def finish(part, coupling, update, panel, slab):
    m, k = panel.shape
    width = slab.shape[1]
    chunks = 16
    return pl.pallas_call(
        functools.partial(finish_kernel, chunks),
        out_shape=(
            jax.ShapeDtypeStruct(part.shape, part.dtype),
            jax.ShapeDtypeStruct(coupling.shape, coupling.dtype),
            jax.ShapeDtypeStruct((m, width), jnp.bfloat16),
        ),
        in_specs=[pl.BlockSpec(memory_space=pltpu.VMEM)] * 5,
        out_specs=[pl.BlockSpec(memory_space=pl.ANY)] * 3,
        scratch_shapes=[pltpu.VMEM((m, width), jnp.bfloat16), pltpu.SemaphoreType.DMA((2 + chunks,))],
        compiler_params=pltpu.CompilerParams(vmem_limit_bytes=12 << 20),
        cost_estimate=pl.CostEstimate(flops=2 * m * k * width, bytes_accessed=2 * m * (k + 2 * width), transcendentals=0),
        name="finish",
    )(part, coupling, update, panel, slab)


def on_device(panel, slab):
    rows, cols = lax.axis_size("row"), lax.axis_size("col")
    there = [pltpu.with_memory_space_constraint(x, pltpu.HBM) for x in (panel, slab)]
    part, coupling, update, panel, slab = solve(*there, rows, cols)
    return finish(part, coupling, update, panel, slab)


def solution(mesh):
    from jax.sharding import PartitionSpec as P

    return jax.shard_map(
        on_device,
        mesh=mesh,
        in_specs=(P("row", None), P("row", "col")),
        out_specs=(P(None, "col"), P(None, "col"), P("row", "col")),
        check_vma=False,
    )
```

```python
import functools

import jax
import jax.numpy as jnp
from jax import lax
from jax.experimental import pallas as pl
from jax.experimental.pallas import tpu as pltpu

HI = lax.Precision.HIGHEST
MESH = pl.DeviceIdType.MESH


def mm(a, b, ca=1, cb=0):
    return lax.dot_general(a, b, (((ca,), (cb,)), ((), ())), precision=HI, preferred_element_type=jnp.float32)


def row_of(x, s):
    return jnp.broadcast_to(x[s : s + 1, :], x.shape)


def lane_of(x, i):
    return jnp.broadcast_to(x[:, i : i + 1], x.shape)


def split3(x):
    hi = x.astype(jnp.bfloat16)
    rest = x - hi.astype(jnp.float32)
    mid = rest.astype(jnp.bfloat16)
    low = (rest - mid.astype(jnp.float32)).astype(jnp.bfloat16)
    return hi, mid, low


def outer(a, b):
    ah, am, al = split3(a)
    bh, bm, bl = split3(b)
    left = jnp.concatenate([ah, ah, am, ah, al, am], axis=0)
    right = jnp.concatenate([bh, bm, bh, bl, bh, bm], axis=0)
    return lax.dot_general(left, right, (((0,), (0,)), ((), ())), preferred_element_type=jnp.float32)


BLOCK, STEP, TILE = 32, 16, 128
PANEL_STEPS = 4


def eliminate(m_ref, r_ref, w_ref, b):
    n = m_ref.shape[1]
    groups = BLOCK // 8
    shape = (8, TILE)
    sub = lax.broadcasted_iota(jnp.int32, shape, 0)
    lane = lax.broadcasted_iota(jnp.int32, shape, 1)
    top = b * BLOCK
    t, lo = top // TILE, top % TILE
    tiles = n // TILE
    inside = (lane >= lo) & (lane < lo + BLOCK)

    def rows(u):
        return [m_ref[top + 8 * g : top + 8 * g + 8, u * TILE : (u + 1) * TILE] for g in range(groups)]

    own = rows(t)
    unit = [jnp.where(inside, jnp.where(lane == sub + (lo + 8 * g), 1.0, 0.0), own[g]) for g in range(groups)]
    other = {u: rows(u) for u in range(tiles) if u != t}
    slabs = [own, unit] + list(other.values())
    for first in range(0, BLOCK, STEP):
        c = [{g: lane_of(own[g], lo + first + k) for g in range((first + k) // 8, groups)} for k in range(STEP)]
        for k in range(STEP):
            gj, sj = divmod(first + k, 8)
            inv = lax.rsqrt(row_of(c[k][gj], sj))
            l = {g: c[k][g] * inv for g in range(gj, groups)}
            for k2 in range(k + 1, STEP):
                g2, s2 = divmod(first + k2, 8)
                at = row_of(l[g2], s2)
                for g in range(g2, groups):
                    c[k2][g] = c[k2][g] - l[g] * at
            below = jnp.where(sub > sj, l[gj], 0.0)
            for x in slabs:
                pivot = row_of(x[gj], sj) * inv
                x[gj] = jnp.where(sub == sj, pivot, x[gj] - below * pivot)
                for g in range(gj + 1, groups):
                    x[g] = x[g] - l[g] * pivot
    zero = jnp.zeros(shape, jnp.float32)
    for g in range(groups):
        at = pl.ds(top + 8 * g, 8)
        for u in range(tiles):
            cols = pl.ds(u * TILE, TILE)
            if u == t:
                r_ref[at, cols] = jnp.where(lane >= sub + (lo + 8 * g), own[g], 0.0)
                w_ref[at, cols] = jnp.where(lane < lo + BLOCK, unit[g], 0.0)
            else:
                r_ref[at, cols] = other[u][g] if u > t else zero
                w_ref[at, cols] = other[u][g] if u < t else zero
    end = top + BLOCK
    if end < n:
        done = jnp.concatenate(
            [jnp.concatenate([unit[g] if u == t else other[u][g] for u in range(tiles)], axis=1) for g in range(groups)], axis=0
        )
        skip = (end // TILE) * TILE
        taken = outer(done[:, skip:], done)
        for u in range(tiles):
            cols = slice(u * TILE, (u + 1) * TILE)
            old = m_ref[end:, cols]
            if u == t:
                wide = lax.broadcasted_iota(jnp.int32, old.shape, 1)
                old = jnp.where((wide >= lo) & (wide < lo + BLOCK), 0.0, old)
            m_ref[end:, cols] = old - taken[end - skip :, cols]


def levels(rows):
    inner = 1
    while inner * inner * 4 <= rows:
        inner *= 2
    return inner, rows // inner


def send(src, dst, sems, index, to_row, to_col):
    copy = pltpu.make_async_remote_copy(
        src_ref=src, dst_ref=dst, send_sem=sems.at[0, index], recv_sem=sems.at[1, index],
        device_id={"row": to_row, "col": to_col}, device_id_type=MESH,
    )
    copy.start()
    return copy


def reduce_all(own, first_in, mid, second_in, result, sems, first, second, col):
    (na, ia, pa, qa), (nb, ib, pb, qb) = first, second
    ra = own.shape[0] // na
    rb = ra // nb
    used = 0

    def to(d, level, src, dst):
        nonlocal used
        used += 1
        return send(src, dst, sems, used - 1, level(d), col)

    sent = []
    for d in reversed(range(1, na)):
        at = pl.multiple_of(qa(d) * ra, 8)
        sent.append(to(d, pa, own.at[pl.ds(at, ra)], first_in.at[d - 1]))
    yield
    here = pl.multiple_of(ia * ra, 8)
    total = own[pl.ds(here, ra), :]
    for d in range(1, na):
        sent[-d].wait()
        total = total + first_in[d - 1]
    sent = []
    if second_in.shape[0] < nb:
        mid[...] = total
        for d in range(1, nb):
            at = pl.multiple_of(qb(d) * rb, 8)
            sent.append(to(d, pb, mid.at[pl.ds(at, rb)], second_in.at[d - 1]))
        yield
        total = mid[pl.ds(pl.multiple_of(ib * rb, 8), rb), :]
        for d in range(1, nb):
            sent[d - 1].wait()
            total = total + second_in[d - 1]
        spot = pl.multiple_of(ia * ra + ib * rb, 8)
        result[pl.ds(spot, rb), :] = total
        sent = []
        for d in range(1, nb):
            part = result.at[pl.ds(spot, rb)]
            sent.append(to(d, pb, part, part))
        yield
        for copy in sent:
            copy.wait()
    else:
        second_in[ib] = total
        for d in range(1, nb):
            sent.append(to(d, pb, second_in.at[ib], second_in.at[ib]))
        yield
        for copy in sent:
            copy.wait()
        total = second_in[0]
        for q in range(1, nb):
            total = total + second_in[q]
        result[pl.ds(here, ra), :] = total
    sent = []
    for d in reversed(range(1, na)):
        part = result.at[pl.ds(here, ra)]
        sent.append(to(d, pa, part, part))
    yield
    for copy in sent:
        copy.wait()
    yield


def reduce_scratch(k, width, na, nb):
    f32 = jnp.float32
    ra = k // na
    rb = ra // nb
    second_in = (max(nb - 1, 1), rb, width) if rb % 8 == 0 else (nb, ra, width)
    return [
        pltpu.VMEM((k, width), f32),
        pltpu.VMEM((max(na - 1, 1), ra, width), f32),
        pltpu.VMEM((ra, width), f32),
        pltpu.VMEM(second_in, f32),
        pltpu.VMEM((k, width), f32),
        pltpu.SemaphoreType.DMA((2, 2 * (na - 1) + 2 * (nb - 1))),
    ]


def stacked(x, axis):
    h, m, l = split3(x)
    return jnp.concatenate([h, h, m, h, l, m] if axis else [h, m, h, l, h, m], axis=axis)


def product(left, right):
    return jnp.dot(left, right, preferred_element_type=jnp.float32)


PLAN = {('start', 0): (0, 1), ('start', 1): (2, 3), 'gram sent': (0, 1), 'gram last': (2, 3, 0, 1), 0: (2,), 1: (0, 3, 1), 4: (2, 3)}
FAR_FIRST = ()


def solve_kernel(
    inner, outer_, cols, split, scale, halves, count, sliced,
    panel_hbm, slab_hbm, part, coupling, update, panel, slab,
    g_own, g_in, g_mid, g_all, m_ref, r_ref, w_ref, panel_sem, slab_sem, g_sem, *cross_refs,
):
    row = lax.axis_index("row")
    col = lax.axis_index("col")
    high, low = row // inner, row % inner
    f32 = jnp.float32
    all_cols = range(cols if split > 1 else 1)

    def other(d):
        at = low
        bit = 1
        while bit < inner:
            if d & bit:
                at = at + bit * (1 - 2 * ((low // bit) % 2))
            bit *= 2
        return at

    def near(d):
        return high * inner + other(d)

    def far(d):
        return ((high + d) % outer_) * inner + low

    def pieces(src, dst, sems):
        rows = src.shape[0] // sems.shape[0]
        parts = [pl.ds(t * rows, rows) for t in range(sems.shape[0])]
        return [pltpu.make_async_copy(src.at[at], dst.at[at], sems.at[t]) for t, at in enumerate(parts)]

    panel_loads = pieces(panel_hbm, panel, panel_sem)
    half = slab.shape[1] // halves
    columns = [(slice(None), pl.ds(t * half, half)) for t in range(halves)]
    slab_loads = [pltpu.make_async_copy(slab_hbm.at[at], slab.at[at], slab_sem.at[t]) for t, at in enumerate(columns)]
    for copy in panel_loads:
        copy.start()

    barrier = pltpu.get_barrier_semaphore()
    greeted = 0
    for d in range(inner):
        for e in all_cols:
            if d or e:
                pl.semaphore_signal(barrier, 1, device_id={"row": near(d), "col": (col + e) % cols}, device_id_type=MESH)
                greeted += 1
    for d in range(1, outer_):
        pl.semaphore_signal(barrier, 1, device_id={"row": far(d), "col": col}, device_id_type=MESH)
        greeted += 1

    def tdot(a, b):
        return lax.dot_general(a, b, (((0,), (0,)), ((), ())), preferred_element_type=f32)

    h = g_own.shape[1]
    chunk = panel.shape[0] // len(panel_loads)
    for t, load in enumerate(panel_loads):
        load.wait()
        if t < len(slab_loads):
            slab_loads[t].start()
        p = panel[t * chunk : (t + 1) * chunk, :]
        top, low_right = tdot(p[:, :h], p), tdot(p[:, h:], p[:, h:])
        acc = (top, low_right) if t == 0 else (acc[0] + top, acc[1] + low_right)
    for copy in slab_loads[len(panel_loads) :]:
        copy.start()
    g_own[:h, :] = acc[0][:, :h] * scale
    g_own[h : 2 * h, :] = acc[0][:, h:] * scale
    g_own[2 * h :, :] = acc[1] * scale

    pl.semaphore_wait(barrier, greeted)

    share = g_own.shape[0] // split
    piece = share // inner
    base = (col * share) if split > 1 else 0
    sent = []
    for d in reversed(range(1, inner)):
        at = pl.multiple_of(base + other(d) * piece, 8)
        sent.append(send(g_own.at[pl.ds(at, piece)], g_in.at[d - 1], g_sem, d - 1, near(d), col))
    used = inner - 1

    ends = ((inner, low, near, other), (outer_, high, far, lambda d: (high + d) % outer_))
    flows = []
    each = count // halves
    width = half // each
    mid = panel.shape[0] // 2

    def advance(point):
        for i in PLAN.get(point, ()):
            if i < len(flows):
                next(flows[i])

    for t, load in enumerate(slab_loads):
        load.wait()
        at = slice(t * half, (t + 1) * half)
        acc = tdot(panel[:mid, :], slab[:mid, at]) + tdot(panel[mid:, :], slab[mid:, at])
        acc = acc * scale
        for i in range(each):
            refs = cross_refs[6 * len(flows) : 6 * len(flows) + 6]
            refs[0][...] = acc[:, i * width : (i + 1) * width]
            order = ends[::-1] if len(flows) in FAR_FIRST else ends
            flows.append(reduce_all(*refs, *order, col))
        advance(("start", t))

    mine = pl.multiple_of(base + low * piece, 8)
    total = g_own[pl.ds(mine, piece), :]
    for d in range(1, inner):
        sent[-d].wait()
        total = total + g_in[d - 1]
    g_mid[high] = total
    sent = []
    for d in range(1, outer_):
        sent.append(send(g_mid.at[high], g_mid.at[high], g_sem, used, far(d), col))
        used += 1
    advance("gram sent")
    for copy in sent:
        copy.wait()
    total = g_mid[0]
    for q in range(1, outer_):
        total = total + g_mid[q]
    g_all[pl.ds(mine, piece), :] = total
    sent = []
    for d in reversed(range(inner)):
        for e in all_cols:
            if d or e:
                at = g_all.at[pl.ds(mine, piece)]
                sent.append(send(at, at, g_sem, used, near(d), (col + e) % cols))
                used += 1
    advance("gram back")
    advance("gram last")
    for copy in sent:
        copy.wait()

    m_ref[:h, :h] = g_all[:h, :]
    m_ref[:h, h:] = g_all[h : 2 * h, :]
    m_ref[h:, h:] = g_all[2 * h :, :]
    m_ref[h:, :h] = jnp.zeros((h, h), f32)
    for b in range(m_ref.shape[0] // BLOCK):
        eliminate(m_ref, r_ref, w_ref, b)
        advance(b)
    share = part.shape[1]
    if sliced:
        part[...] = r_ref[:, pl.ds(pl.multiple_of(col * share, TILE), share)]
    else:
        part[...] = r_ref[...]

    w = w_ref[...]
    both = stacked(w, 1), stacked(product(stacked(w.T, 1), stacked(w, 0)), 1)
    for t in range(halves):
        at = slice(t * half, (t + 1) * half)
        for flow in flows[t * each : (t + 1) * each]:
            for _ in flow:
                pass
        cross = jnp.concatenate([cross_refs[6 * i + 4][...] for i in range(t * each, (t + 1) * each)], axis=1)
        right = stacked(cross, 0)
        x, z = (product(left, right) for left in both)
        coupling[:, at] = x
        update[:, at] = z.astype(jnp.bfloat16)


def solve(panel, slab, rows, cols):
    m, k = panel.shape
    width = slab.shape[1]
    inner, outer_ = levels(rows)
    h = k // 2
    split = cols if (3 * h) % (8 * inner * cols) == 0 else 1
    piece = 3 * h // split // inner
    sliced = (k // cols) % TILE == 0
    share = k // cols if sliced else k
    f32, bf16 = jnp.float32, jnp.bfloat16
    halves = 2 if width % (4 * TILE) == 0 else 1
    count = 4 if halves == 2 and k % (8 * rows) == 0 else halves
    g_copies = (inner - 1) + (outer_ - 1) + inner * (cols if split > 1 else 1) - 1
    hbm = pl.BlockSpec(memory_space=pl.ANY)
    scratch = [
        pltpu.VMEM((3 * h, h), f32),
        pltpu.VMEM((max(inner - 1, 1), piece, h), f32),
        pltpu.VMEM((outer_, piece, h), f32),
        pltpu.VMEM((3 * h, h), f32),
        pltpu.VMEM((k, k), f32),
        pltpu.VMEM((k, k), f32),
        pltpu.VMEM((k, k), f32),
        pltpu.SemaphoreType.DMA((PANEL_STEPS,)),
        pltpu.SemaphoreType.DMA((halves,)),
        pltpu.SemaphoreType.DMA((2, g_copies)),
    ]
    for i in range(count):
        scratch += reduce_scratch(k, width // count, *((outer_, inner) if i in FAR_FIRST else (inner, outer_)))
    part, coupling, update, panel, slab = pl.pallas_call(
        functools.partial(solve_kernel, inner, outer_, cols, split, 1.0 / (m * rows), halves, count, sliced),
        out_shape=(
            jax.ShapeDtypeStruct((k, share), f32),
            jax.ShapeDtypeStruct((k, width), f32),
            jax.ShapeDtypeStruct((k, width), bf16),
            jax.ShapeDtypeStruct((m, k), bf16),
            jax.ShapeDtypeStruct((m, width), bf16),
        ),
        in_specs=[hbm, hbm],
        out_specs=[pl.BlockSpec(memory_space=pltpu.VMEM)] * 5,
        scratch_shapes=scratch,
        compiler_params=pltpu.CompilerParams(collective_id=0, has_side_effects=True, vmem_limit_bytes=20 << 20),
        cost_estimate=pl.CostEstimate(flops=2 * m * k * (k + width), bytes_accessed=2 * m * (k + width), transcendentals=0),
        name="solve",
    )(panel, slab)
    if not sliced:
        part = lax.dynamic_slice_in_dim(part, lax.axis_index("col") * (k // cols), k // cols, 1)
    return part, coupling, update, panel, slab


def finish_kernel(chunks, part, coupling, update, panel, slab, part_out, coupling_out, out, kept, sems):
    copies = [
        pltpu.make_async_copy(coupling, coupling_out, sems.at[0]),
        pltpu.make_async_copy(part, part_out, sems.at[1]),
    ]
    for copy in copies:
        copy.start()
    rows = panel.shape[0] // chunks
    z = update[...]
    for t in range(chunks):
        at = pl.ds(t * rows, rows)
        taken = jnp.dot(panel[at, :], z, preferred_element_type=jnp.float32)
        kept[at, :] = (slab[at, :].astype(jnp.float32) - taken).astype(jnp.bfloat16)
        copies.append(pltpu.make_async_copy(kept.at[at], out.at[at], sems.at[2 + t]))
        copies[-1].start()
    for copy in copies:
        copy.wait()


def finish(part, coupling, update, panel, slab):
    m, k = panel.shape
    width = slab.shape[1]
    chunks = 16
    return pl.pallas_call(
        functools.partial(finish_kernel, chunks),
        out_shape=(
            jax.ShapeDtypeStruct(part.shape, part.dtype),
            jax.ShapeDtypeStruct(coupling.shape, coupling.dtype),
            jax.ShapeDtypeStruct((m, width), jnp.bfloat16),
        ),
        in_specs=[pl.BlockSpec(memory_space=pltpu.VMEM)] * 5,
        out_specs=[pl.BlockSpec(memory_space=pl.ANY)] * 3,
        scratch_shapes=[pltpu.VMEM((m, width), jnp.bfloat16), pltpu.SemaphoreType.DMA((2 + chunks,))],
        compiler_params=pltpu.CompilerParams(vmem_limit_bytes=12 << 20),
        cost_estimate=pl.CostEstimate(flops=2 * m * k * width, bytes_accessed=2 * m * (k + 2 * width), transcendentals=0),
        name="finish",
    )(part, coupling, update, panel, slab)


def on_device(panel, slab):
    rows, cols = lax.axis_size("row"), lax.axis_size("col")
    there = [pltpu.with_memory_space_constraint(x, pltpu.HBM) for x in (panel, slab)]
    part, coupling, update, panel, slab = solve(*there, rows, cols)
    return finish(part, coupling, update, panel, slab)


def solution(mesh):
    from jax.sharding import PartitionSpec as P

    return jax.shard_map(
        on_device,
        mesh=mesh,
        in_specs=(P("row", None), P("row", "col")),
        out_specs=(P(None, "col"), P(None, "col"), P("row", "col")),
        check_vma=False,
    )
```

```python
import functools

import jax
import jax.numpy as jnp
from jax import lax
from jax.experimental import pallas as pl
from jax.experimental.pallas import tpu as pltpu

HI = lax.Precision.HIGHEST
MESH = pl.DeviceIdType.MESH


def mm(a, b, ca=1, cb=0):
    return lax.dot_general(a, b, (((ca,), (cb,)), ((), ())), precision=HI, preferred_element_type=jnp.float32)


def row_of(x, s):
    return jnp.broadcast_to(x[s : s + 1, :], x.shape)


def lane_of(x, i):
    return jnp.broadcast_to(x[:, i : i + 1], x.shape)


def split3(x):
    hi = x.astype(jnp.bfloat16)
    rest = x - hi.astype(jnp.float32)
    mid = rest.astype(jnp.bfloat16)
    low = (rest - mid.astype(jnp.float32)).astype(jnp.bfloat16)
    return hi, mid, low


def outer(a, b):
    ah, am, al = split3(a)
    bh, bm, bl = split3(b)
    left = jnp.concatenate([ah, ah, am, ah, al, am], axis=0)
    right = jnp.concatenate([bh, bm, bh, bl, bh, bm], axis=0)
    return lax.dot_general(left, right, (((0,), (0,)), ((), ())), preferred_element_type=jnp.float32)


BLOCK, STEP, TILE = 32, 16, 128
PANEL_STEPS = 4


def eliminate(m_ref, r_ref, w_ref, b):
    n = m_ref.shape[1]
    groups = BLOCK // 8
    shape = (8, TILE)
    sub = lax.broadcasted_iota(jnp.int32, shape, 0)
    lane = lax.broadcasted_iota(jnp.int32, shape, 1)
    top = b * BLOCK
    t, lo = top // TILE, top % TILE
    tiles = n // TILE
    inside = (lane >= lo) & (lane < lo + BLOCK)

    def rows(u):
        return [m_ref[top + 8 * g : top + 8 * g + 8, u * TILE : (u + 1) * TILE] for g in range(groups)]

    own = rows(t)
    unit = [jnp.where(inside, jnp.where(lane == sub + (lo + 8 * g), 1.0, 0.0), own[g]) for g in range(groups)]
    other = {u: rows(u) for u in range(tiles) if u != t}
    slabs = [own, unit] + list(other.values())
    for first in range(0, BLOCK, STEP):
        c = [{g: lane_of(own[g], lo + first + k) for g in range((first + k) // 8, groups)} for k in range(STEP)]
        for k in range(STEP):
            gj, sj = divmod(first + k, 8)
            inv = lax.rsqrt(row_of(c[k][gj], sj))
            l = {g: c[k][g] * inv for g in range(gj, groups)}
            for k2 in range(k + 1, STEP):
                g2, s2 = divmod(first + k2, 8)
                at = row_of(l[g2], s2)
                for g in range(g2, groups):
                    c[k2][g] = c[k2][g] - l[g] * at
            below = jnp.where(sub > sj, l[gj], 0.0)
            for x in slabs:
                pivot = row_of(x[gj], sj) * inv
                x[gj] = jnp.where(sub == sj, pivot, x[gj] - below * pivot)
                for g in range(gj + 1, groups):
                    x[g] = x[g] - l[g] * pivot
    zero = jnp.zeros(shape, jnp.float32)
    for g in range(groups):
        at = pl.ds(top + 8 * g, 8)
        for u in range(tiles):
            cols = pl.ds(u * TILE, TILE)
            if u == t:
                r_ref[at, cols] = jnp.where(lane >= sub + (lo + 8 * g), own[g], 0.0)
                w_ref[at, cols] = jnp.where(lane < lo + BLOCK, unit[g], 0.0)
            else:
                r_ref[at, cols] = other[u][g] if u > t else zero
                w_ref[at, cols] = other[u][g] if u < t else zero
    end = top + BLOCK
    if end < n:
        done = jnp.concatenate(
            [jnp.concatenate([unit[g] if u == t else other[u][g] for u in range(tiles)], axis=1) for g in range(groups)], axis=0
        )
        skip = (end // TILE) * TILE
        taken = outer(done[:, skip:], done)
        for u in range(tiles):
            cols = slice(u * TILE, (u + 1) * TILE)
            old = m_ref[end:, cols]
            if u == t:
                wide = lax.broadcasted_iota(jnp.int32, old.shape, 1)
                old = jnp.where((wide >= lo) & (wide < lo + BLOCK), 0.0, old)
            m_ref[end:, cols] = old - taken[end - skip :, cols]


def levels(rows):
    inner = 1
    while inner * inner * 4 <= rows:
        inner *= 2
    return inner, rows // inner


def send(src, dst, sems, index, to_row, to_col):
    copy = pltpu.make_async_remote_copy(
        src_ref=src, dst_ref=dst, send_sem=sems.at[0, index], recv_sem=sems.at[1, index],
        device_id={"row": to_row, "col": to_col}, device_id_type=MESH,
    )
    copy.start()
    return copy


def reduce_all(own, first_in, mid, second_in, result, sems, first, second, col):
    (na, ia, pa, qa), (nb, ib, pb, qb) = first, second
    ra = own.shape[0] // na
    rb = ra // nb
    used = 0

    def to(d, level, src, dst):
        nonlocal used
        used += 1
        return send(src, dst, sems, used - 1, level(d), col)

    sent = []
    for d in reversed(range(1, na)):
        at = pl.multiple_of(qa(d) * ra, 8)
        sent.append(to(d, pa, own.at[pl.ds(at, ra)], first_in.at[d - 1]))
    yield
    here = pl.multiple_of(ia * ra, 8)
    total = own[pl.ds(here, ra), :]
    for d in range(1, na):
        sent[-d].wait()
        total = total + first_in[d - 1]
    sent = []
    if second_in.shape[0] < nb:
        mid[...] = total
        for d in range(1, nb):
            at = pl.multiple_of(qb(d) * rb, 8)
            sent.append(to(d, pb, mid.at[pl.ds(at, rb)], second_in.at[d - 1]))
        yield
        total = mid[pl.ds(pl.multiple_of(ib * rb, 8), rb), :]
        for d in range(1, nb):
            sent[d - 1].wait()
            total = total + second_in[d - 1]
        spot = pl.multiple_of(ia * ra + ib * rb, 8)
        result[pl.ds(spot, rb), :] = total
        sent = []
        for d in range(1, nb):
            part = result.at[pl.ds(spot, rb)]
            sent.append(to(d, pb, part, part))
        yield
        for copy in sent:
            copy.wait()
    else:
        second_in[ib] = total
        for d in range(1, nb):
            sent.append(to(d, pb, second_in.at[ib], second_in.at[ib]))
        yield
        for copy in sent:
            copy.wait()
        total = second_in[0]
        for q in range(1, nb):
            total = total + second_in[q]
        result[pl.ds(here, ra), :] = total
    sent = []
    for d in reversed(range(1, na)):
        part = result.at[pl.ds(here, ra)]
        sent.append(to(d, pa, part, part))
    yield
    for copy in sent:
        copy.wait()
    yield


def reduce_scratch(k, width, na, nb):
    f32 = jnp.float32
    ra = k // na
    rb = ra // nb
    second_in = (max(nb - 1, 1), rb, width) if rb % 8 == 0 else (nb, ra, width)
    return [
        pltpu.VMEM((k, width), f32),
        pltpu.VMEM((max(na - 1, 1), ra, width), f32),
        pltpu.VMEM((ra, width), f32),
        pltpu.VMEM(second_in, f32),
        pltpu.VMEM((k, width), f32),
        pltpu.SemaphoreType.DMA((2, 2 * (na - 1) + 2 * (nb - 1))),
    ]


def stacked(x, axis):
    h, m, l = split3(x)
    return jnp.concatenate([h, h, m, h, l, m] if axis else [h, m, h, l, h, m], axis=axis)


def product(left, right):
    return jnp.dot(left, right, preferred_element_type=jnp.float32)


PLAN = {('start', 0): (0, 1), ('start', 1): (2, 3), 'gram sent': (0, 1), 'gram last': (2, 3, 0, 1), 0: (2,), 1: (0, 3, 1), 4: (2, 3)}
FAR_FIRST = ()


def solve_kernel(
    inner, outer_, cols, split, scale, halves, count, sliced,
    panel_hbm, slab_hbm, part, coupling, update, panel, slab,
    g_own, g_in, g_mid, g_all, m_ref, r_ref, w_ref, panel_sem, slab_sem, g_sem, *cross_refs,
):
    row = lax.axis_index("row")
    col = lax.axis_index("col")
    high, low = row // inner, row % inner
    f32 = jnp.float32
    all_cols = range(cols if split > 1 else 1)

    def other(d):
        at = low
        bit = 1
        while bit < inner:
            if d & bit:
                at = at + bit * (1 - 2 * ((low // bit) % 2))
            bit *= 2
        return at

    def near(d):
        return high * inner + other(d)

    def far(d):
        return ((high + d) % outer_) * inner + low

    def pieces(src, dst, sems):
        rows = src.shape[0] // sems.shape[0]
        parts = [pl.ds(t * rows, rows) for t in range(sems.shape[0])]
        return [pltpu.make_async_copy(src.at[at], dst.at[at], sems.at[t]) for t, at in enumerate(parts)]

    panel_loads = pieces(panel_hbm, panel, panel_sem)
    half = slab.shape[1] // halves
    columns = [(slice(None), pl.ds(t * half, half)) for t in range(halves)]
    slab_loads = [pltpu.make_async_copy(slab_hbm.at[at], slab.at[at], slab_sem.at[t]) for t, at in enumerate(columns)]
    for copy in panel_loads:
        copy.start()

    barrier = pltpu.get_barrier_semaphore()
    greeted = 0
    for d in range(inner):
        for e in all_cols:
            if d or e:
                pl.semaphore_signal(barrier, 1, device_id={"row": near(d), "col": (col + e) % cols}, device_id_type=MESH)
                greeted += 1
    for d in range(1, outer_):
        pl.semaphore_signal(barrier, 1, device_id={"row": far(d), "col": col}, device_id_type=MESH)
        greeted += 1

    def tdot(a, b):
        return lax.dot_general(a, b, (((0,), (0,)), ((), ())), preferred_element_type=f32)

    h = g_own.shape[1]
    chunk = panel.shape[0] // len(panel_loads)
    for t, load in enumerate(panel_loads):
        load.wait()
        if t == 0:
            for copy in slab_loads:
                copy.start()
        p = panel[t * chunk : (t + 1) * chunk, :]
        top, low_right = tdot(p[:, :h], p), tdot(p[:, h:], p[:, h:])
        acc = (top, low_right) if t == 0 else (acc[0] + top, acc[1] + low_right)
    g_own[:h, :] = acc[0][:, :h] * scale
    g_own[h : 2 * h, :] = acc[0][:, h:] * scale
    g_own[2 * h :, :] = acc[1] * scale

    pl.semaphore_wait(barrier, greeted)

    share = g_own.shape[0] // split
    piece = share // inner
    base = (col * share) if split > 1 else 0
    sent = []
    for d in reversed(range(1, inner)):
        at = pl.multiple_of(base + other(d) * piece, 8)
        sent.append(send(g_own.at[pl.ds(at, piece)], g_in.at[d - 1], g_sem, d - 1, near(d), col))
    used = inner - 1

    ends = ((inner, low, near, other), (outer_, high, far, lambda d: (high + d) % outer_))
    flows = []
    each = count // halves
    width = half // each
    mid = panel.shape[0] // 2

    def advance(point):
        for i in PLAN.get(point, ()):
            if i < len(flows):
                next(flows[i])

    for t, load in enumerate(slab_loads):
        load.wait()
        at = slice(t * half, (t + 1) * half)
        acc = tdot(panel[:mid, :], slab[:mid, at]) + tdot(panel[mid:, :], slab[mid:, at])
        acc = acc * scale
        for i in range(each):
            refs = cross_refs[6 * len(flows) : 6 * len(flows) + 6]
            refs[0][...] = acc[:, i * width : (i + 1) * width]
            order = ends[::-1] if len(flows) in FAR_FIRST else ends
            flows.append(reduce_all(*refs, *order, col))
        advance(("start", t))

    mine = pl.multiple_of(base + low * piece, 8)
    total = g_own[pl.ds(mine, piece), :]
    for d in range(1, inner):
        sent[-d].wait()
        total = total + g_in[d - 1]
    g_mid[high] = total
    sent = []
    for d in range(1, outer_):
        sent.append(send(g_mid.at[high], g_mid.at[high], g_sem, used, far(d), col))
        used += 1
    advance("gram sent")
    for copy in sent:
        copy.wait()
    total = g_mid[0]
    for q in range(1, outer_):
        total = total + g_mid[q]
    g_all[pl.ds(mine, piece), :] = total
    sent = []
    for d in reversed(range(inner)):
        for e in all_cols:
            if d or e:
                at = g_all.at[pl.ds(mine, piece)]
                sent.append(send(at, at, g_sem, used, near(d), (col + e) % cols))
                used += 1
    m_ref[h:, :h] = jnp.zeros((h, h), f32)
    advance("gram back")
    advance("gram last")
    for copy in sent:
        copy.wait()

    m_ref[:h, :h] = g_all[:h, :]
    m_ref[:h, h:] = g_all[h : 2 * h, :]
    m_ref[h:, h:] = g_all[2 * h :, :]
    for b in range(m_ref.shape[0] // BLOCK):
        eliminate(m_ref, r_ref, w_ref, b)
        advance(b)
    w = w_ref[...]
    both = stacked(w, 1), stacked(product(stacked(w.T, 1), stacked(w, 0)), 1)
    for t in range(halves):
        at = slice(t * half, (t + 1) * half)
        for flow in flows[t * each : (t + 1) * each]:
            for _ in flow:
                pass
        cross = jnp.concatenate([cross_refs[6 * i + 4][...] for i in range(t * each, (t + 1) * each)], axis=1)
        right = stacked(cross, 0)
        x, z = (product(left, right) for left in both)
        coupling[:, at] = x
        update[:, at] = z.astype(jnp.bfloat16)
        if t == 0:
            share = part.shape[1]
            if sliced:
                part[...] = r_ref[:, pl.ds(pl.multiple_of(col * share, TILE), share)]
            else:
                part[...] = r_ref[...]


def solve(panel, slab, rows, cols):
    m, k = panel.shape
    width = slab.shape[1]
    inner, outer_ = levels(rows)
    h = k // 2
    split = cols if (3 * h) % (8 * inner * cols) == 0 else 1
    piece = 3 * h // split // inner
    sliced = (k // cols) % TILE == 0
    share = k // cols if sliced else k
    f32, bf16 = jnp.float32, jnp.bfloat16
    halves = 2 if width % (4 * TILE) == 0 else 1
    count = 4 if halves == 2 and k % (8 * rows) == 0 else halves
    g_copies = (inner - 1) + (outer_ - 1) + inner * (cols if split > 1 else 1) - 1
    hbm = pl.BlockSpec(memory_space=pl.ANY)
    scratch = [
        pltpu.VMEM((3 * h, h), f32),
        pltpu.VMEM((max(inner - 1, 1), piece, h), f32),
        pltpu.VMEM((outer_, piece, h), f32),
        pltpu.VMEM((3 * h, h), f32),
        pltpu.VMEM((k, k), f32),
        pltpu.VMEM((k, k), f32),
        pltpu.VMEM((k, k), f32),
        pltpu.SemaphoreType.DMA((PANEL_STEPS,)),
        pltpu.SemaphoreType.DMA((halves,)),
        pltpu.SemaphoreType.DMA((2, g_copies)),
    ]
    for i in range(count):
        scratch += reduce_scratch(k, width // count, *((outer_, inner) if i in FAR_FIRST else (inner, outer_)))
    part, coupling, update, panel, slab = pl.pallas_call(
        functools.partial(solve_kernel, inner, outer_, cols, split, 1.0 / (m * rows), halves, count, sliced),
        out_shape=(
            jax.ShapeDtypeStruct((k, share), f32),
            jax.ShapeDtypeStruct((k, width), f32),
            jax.ShapeDtypeStruct((k, width), bf16),
            jax.ShapeDtypeStruct((m, k), bf16),
            jax.ShapeDtypeStruct((m, width), bf16),
        ),
        in_specs=[hbm, hbm],
        out_specs=[pl.BlockSpec(memory_space=pltpu.VMEM)] * 5,
        scratch_shapes=scratch,
        compiler_params=pltpu.CompilerParams(collective_id=0, has_side_effects=True, vmem_limit_bytes=20 << 20),
        cost_estimate=pl.CostEstimate(flops=2 * m * k * (k + width), bytes_accessed=2 * m * (k + width), transcendentals=0),
        name="solve",
    )(panel, slab)
    if not sliced:
        part = lax.dynamic_slice_in_dim(part, lax.axis_index("col") * (k // cols), k // cols, 1)
    return part, coupling, update, panel, slab


def finish_kernel(chunks, part, coupling, update, panel, slab, part_out, coupling_out, out, kept, sems):
    copies = [
        pltpu.make_async_copy(coupling, coupling_out, sems.at[0]),
        pltpu.make_async_copy(part, part_out, sems.at[1]),
    ]
    for copy in copies:
        copy.start()
    rows = panel.shape[0] // chunks
    z = update[...]
    for t in range(chunks):
        at = pl.ds(t * rows, rows)
        taken = jnp.dot(panel[at, :], z, preferred_element_type=jnp.float32)
        kept[at, :] = (slab[at, :].astype(jnp.float32) - taken).astype(jnp.bfloat16)
        copies.append(pltpu.make_async_copy(kept.at[at], out.at[at], sems.at[2 + t]))
        copies[-1].start()
    for copy in copies:
        copy.wait()


def finish(part, coupling, update, panel, slab):
    m, k = panel.shape
    width = slab.shape[1]
    chunks = 16
    return pl.pallas_call(
        functools.partial(finish_kernel, chunks),
        out_shape=(
            jax.ShapeDtypeStruct(part.shape, part.dtype),
            jax.ShapeDtypeStruct(coupling.shape, coupling.dtype),
            jax.ShapeDtypeStruct((m, width), jnp.bfloat16),
        ),
        in_specs=[pl.BlockSpec(memory_space=pltpu.VMEM)] * 5,
        out_specs=[pl.BlockSpec(memory_space=pl.ANY)] * 3,
        scratch_shapes=[pltpu.VMEM((m, width), jnp.bfloat16), pltpu.SemaphoreType.DMA((2 + chunks,))],
        compiler_params=pltpu.CompilerParams(vmem_limit_bytes=12 << 20),
        cost_estimate=pl.CostEstimate(flops=2 * m * k * width, bytes_accessed=2 * m * (k + 2 * width), transcendentals=0),
        name="finish",
    )(part, coupling, update, panel, slab)


def on_device(panel, slab):
    rows, cols = lax.axis_size("row"), lax.axis_size("col")
    there = [pltpu.with_memory_space_constraint(x, pltpu.HBM) for x in (panel, slab)]
    part, coupling, update, panel, slab = solve(*there, rows, cols)
    return finish(part, coupling, update, panel, slab)


def solution(mesh):
    from jax.sharding import PartitionSpec as P

    return jax.shard_map(
        on_device,
        mesh=mesh,
        in_specs=(P("row", None), P("row", "col")),
        out_specs=(P(None, "col"), P(None, "col"), P("row", "col")),
        check_vma=False,
    )
```

```python
import functools

import jax
import jax.numpy as jnp
from jax import lax
from jax.experimental import pallas as pl
from jax.experimental.pallas import tpu as pltpu

HI = lax.Precision.HIGHEST
MESH = pl.DeviceIdType.MESH


def mm(a, b, ca=1, cb=0):
    return lax.dot_general(a, b, (((ca,), (cb,)), ((), ())), precision=HI, preferred_element_type=jnp.float32)


def row_of(x, s):
    return jnp.broadcast_to(x[s : s + 1, :], x.shape)


def lane_of(x, i):
    return jnp.broadcast_to(x[:, i : i + 1], x.shape)


def split3(x):
    hi = x.astype(jnp.bfloat16)
    rest = x - hi.astype(jnp.float32)
    mid = rest.astype(jnp.bfloat16)
    low = (rest - mid.astype(jnp.float32)).astype(jnp.bfloat16)
    return hi, mid, low


def outer(a, b):
    ah, am, al = split3(a)
    bh, bm, bl = split3(b)
    left = jnp.concatenate([ah, ah, am, ah, al, am], axis=0)
    right = jnp.concatenate([bh, bm, bh, bl, bh, bm], axis=0)
    return lax.dot_general(left, right, (((0,), (0,)), ((), ())), preferred_element_type=jnp.float32)


BLOCK, STEP, TILE = 32, 16, 128
PANEL_STEPS = 4


def eliminate(m_ref, r_ref, w_ref, b):
    n = m_ref.shape[1]
    groups = BLOCK // 8
    shape = (8, TILE)
    sub = lax.broadcasted_iota(jnp.int32, shape, 0)
    lane = lax.broadcasted_iota(jnp.int32, shape, 1)
    top = b * BLOCK
    t, lo = top // TILE, top % TILE
    tiles = n // TILE
    inside = (lane >= lo) & (lane < lo + BLOCK)

    def rows(u):
        return [m_ref[top + 8 * g : top + 8 * g + 8, u * TILE : (u + 1) * TILE] for g in range(groups)]

    own = rows(t)
    unit = [jnp.where(inside, jnp.where(lane == sub + (lo + 8 * g), 1.0, 0.0), own[g]) for g in range(groups)]
    other = {u: rows(u) for u in range(tiles) if u != t}
    slabs = [own, unit] + list(other.values())
    for first in range(0, BLOCK, STEP):
        c = [{g: lane_of(own[g], lo + first + k) for g in range((first + k) // 8, groups)} for k in range(STEP)]
        for k in range(STEP):
            gj, sj = divmod(first + k, 8)
            inv = lax.rsqrt(row_of(c[k][gj], sj))
            l = {g: c[k][g] * inv for g in range(gj, groups)}
            for k2 in range(k + 1, STEP):
                g2, s2 = divmod(first + k2, 8)
                at = row_of(l[g2], s2)
                for g in range(g2, groups):
                    c[k2][g] = c[k2][g] - l[g] * at
            below = jnp.where(sub > sj, l[gj], 0.0)
            for x in slabs:
                pivot = row_of(x[gj], sj) * inv
                x[gj] = jnp.where(sub == sj, pivot, x[gj] - below * pivot)
                for g in range(gj + 1, groups):
                    x[g] = x[g] - l[g] * pivot
    zero = jnp.zeros(shape, jnp.float32)
    for g in range(groups):
        at = pl.ds(top + 8 * g, 8)
        for u in range(tiles):
            cols = pl.ds(u * TILE, TILE)
            if u == t:
                r_ref[at, cols] = jnp.where(lane >= sub + (lo + 8 * g), own[g], 0.0)
                w_ref[at, cols] = jnp.where(lane < lo + BLOCK, unit[g], 0.0)
            else:
                r_ref[at, cols] = other[u][g] if u > t else zero
                w_ref[at, cols] = other[u][g] if u < t else zero
    end = top + BLOCK
    if end < n:
        done = jnp.concatenate(
            [jnp.concatenate([unit[g] if u == t else other[u][g] for u in range(tiles)], axis=1) for g in range(groups)], axis=0
        )
        skip = (end // TILE) * TILE
        taken = outer(done[:, skip:], done)
        for u in range(tiles):
            cols = slice(u * TILE, (u + 1) * TILE)
            old = m_ref[end:, cols]
            if u == t:
                wide = lax.broadcasted_iota(jnp.int32, old.shape, 1)
                old = jnp.where((wide >= lo) & (wide < lo + BLOCK), 0.0, old)
            m_ref[end:, cols] = old - taken[end - skip :, cols]


def levels(rows):
    inner = 1
    while inner * inner * 4 <= rows:
        inner *= 2
    return inner, rows // inner


def send(src, dst, sems, index, to_row, to_col):
    copy = pltpu.make_async_remote_copy(
        src_ref=src, dst_ref=dst, send_sem=sems.at[0, index], recv_sem=sems.at[1, index],
        device_id={"row": to_row, "col": to_col}, device_id_type=MESH,
    )
    copy.start()
    return copy


def reduce_all(own, first_in, mid, second_in, result, sems, first, second, col):
    (na, ia, pa, qa), (nb, ib, pb, qb) = first, second
    ra = own.shape[0] // na
    rb = ra // nb
    used = 0

    def to(d, level, src, dst):
        nonlocal used
        used += 1
        return send(src, dst, sems, used - 1, level(d), col)

    sent = []
    for d in reversed(range(1, na)):
        at = pl.multiple_of(qa(d) * ra, 8)
        sent.append(to(d, pa, own.at[pl.ds(at, ra)], first_in.at[d - 1]))
    yield
    here = pl.multiple_of(ia * ra, 8)
    total = own[pl.ds(here, ra), :]
    for d in range(1, na):
        sent[-d].wait()
        total = total + first_in[d - 1]
    sent = []
    if second_in.shape[0] < nb:
        mid[...] = total
        for d in range(1, nb):
            at = pl.multiple_of(qb(d) * rb, 8)
            sent.append(to(d, pb, mid.at[pl.ds(at, rb)], second_in.at[d - 1]))
        yield
        total = mid[pl.ds(pl.multiple_of(ib * rb, 8), rb), :]
        for d in range(1, nb):
            sent[d - 1].wait()
            total = total + second_in[d - 1]
        spot = pl.multiple_of(ia * ra + ib * rb, 8)
        result[pl.ds(spot, rb), :] = total
        sent = []
        for d in range(1, nb):
            part = result.at[pl.ds(spot, rb)]
            sent.append(to(d, pb, part, part))
        yield
        for copy in sent:
            copy.wait()
    else:
        second_in[ib] = total
        for d in range(1, nb):
            sent.append(to(d, pb, second_in.at[ib], second_in.at[ib]))
        yield
        for copy in sent:
            copy.wait()
        total = second_in[0]
        for q in range(1, nb):
            total = total + second_in[q]
        result[pl.ds(here, ra), :] = total
    sent = []
    for d in reversed(range(1, na)):
        part = result.at[pl.ds(here, ra)]
        sent.append(to(d, pa, part, part))
    yield
    for copy in sent:
        copy.wait()
    yield


def reduce_scratch(k, width, na, nb):
    f32 = jnp.float32
    ra = k // na
    rb = ra // nb
    second_in = (max(nb - 1, 1), rb, width) if rb % 8 == 0 else (nb, ra, width)
    return [
        pltpu.VMEM((k, width), f32),
        pltpu.VMEM((max(na - 1, 1), ra, width), f32),
        pltpu.VMEM((ra, width), f32),
        pltpu.VMEM(second_in, f32),
        pltpu.VMEM((k, width), f32),
        pltpu.SemaphoreType.DMA((2, 2 * (na - 1) + 2 * (nb - 1))),
    ]


def stacked(x, axis):
    h, m, l = split3(x)
    return jnp.concatenate([h, h, m, h, l, m] if axis else [h, m, h, l, h, m], axis=axis)


def product(left, right):
    mid = left.shape[0] // 2
    halves = (jnp.dot(part, right, preferred_element_type=jnp.float32) for part in (left[:mid, :], left[mid:, :]))
    return jnp.concatenate(list(halves), axis=0)


PLAN = {('start', 0): (0, 1), ('start', 1): (2, 3), 'gram sent': (0, 1), 'gram last': (2, 3, 0, 1), 0: (2,), 1: (0, 3, 1), 4: (2, 3)}
FAR_FIRST = ()


def solve_kernel(
    inner, outer_, cols, split, scale, halves, count, sliced,
    panel_hbm, slab_hbm, part, coupling, update, panel, slab,
    g_own, g_in, g_mid, g_all, m_ref, r_ref, w_ref, panel_sem, slab_sem, g_sem, *cross_refs,
):
    row = lax.axis_index("row")
    col = lax.axis_index("col")
    high, low = row // inner, row % inner
    f32 = jnp.float32
    all_cols = range(cols if split > 1 else 1)

    def other(d):
        at = low
        bit = 1
        while bit < inner:
            if d & bit:
                at = at + bit * (1 - 2 * ((low // bit) % 2))
            bit *= 2
        return at

    def near(d):
        return high * inner + other(d)

    def far(d):
        return ((high + d) % outer_) * inner + low

    def pieces(src, dst, sems):
        rows = src.shape[0] // sems.shape[0]
        parts = [pl.ds(t * rows, rows) for t in range(sems.shape[0])]
        return [pltpu.make_async_copy(src.at[at], dst.at[at], sems.at[t]) for t, at in enumerate(parts)]

    panel_loads = pieces(panel_hbm, panel, panel_sem)
    half = slab.shape[1] // halves
    columns = [(slice(None), pl.ds(t * half, half)) for t in range(halves)]
    slab_loads = [pltpu.make_async_copy(slab_hbm.at[at], slab.at[at], slab_sem.at[t]) for t, at in enumerate(columns)]
    for copy in panel_loads:
        copy.start()

    barrier = pltpu.get_barrier_semaphore()
    greeted = 0
    for d in range(inner):
        for e in all_cols:
            if d or e:
                pl.semaphore_signal(barrier, 1, device_id={"row": near(d), "col": (col + e) % cols}, device_id_type=MESH)
                greeted += 1
    for d in range(1, outer_):
        pl.semaphore_signal(barrier, 1, device_id={"row": far(d), "col": col}, device_id_type=MESH)
        greeted += 1

    def tdot(a, b):
        return lax.dot_general(a, b, (((0,), (0,)), ((), ())), preferred_element_type=f32)

    h = g_own.shape[1]
    chunk = panel.shape[0] // len(panel_loads)
    for t, load in enumerate(panel_loads):
        load.wait()
        if t < len(slab_loads):
            slab_loads[t].start()
        p = panel[t * chunk : (t + 1) * chunk, :]
        top, low_right = tdot(p[:, :h], p), tdot(p[:, h:], p[:, h:])
        acc = (top, low_right) if t == 0 else (acc[0] + top, acc[1] + low_right)
    for copy in slab_loads[len(panel_loads) :]:
        copy.start()
    g_own[:h, :] = acc[0][:, :h] * scale
    g_own[h : 2 * h, :] = acc[0][:, h:] * scale
    g_own[2 * h :, :] = acc[1] * scale

    pl.semaphore_wait(barrier, greeted)

    share = g_own.shape[0] // split
    piece = share // inner
    base = (col * share) if split > 1 else 0
    sent = []
    for d in reversed(range(1, inner)):
        at = pl.multiple_of(base + other(d) * piece, 8)
        sent.append(send(g_own.at[pl.ds(at, piece)], g_in.at[d - 1], g_sem, d - 1, near(d), col))
    used = inner - 1

    ends = ((inner, low, near, other), (outer_, high, far, lambda d: (high + d) % outer_))
    flows = []
    each = count // halves
    width = half // each
    mid = panel.shape[0] // 2

    def advance(point):
        for i in PLAN.get(point, ()):
            if i < len(flows):
                next(flows[i])

    for t, load in enumerate(slab_loads):
        load.wait()
        at = slice(t * half, (t + 1) * half)
        acc = tdot(panel[:mid, :], slab[:mid, at]) + tdot(panel[mid:, :], slab[mid:, at])
        acc = acc * scale
        for i in range(each):
            refs = cross_refs[6 * len(flows) : 6 * len(flows) + 6]
            refs[0][...] = acc[:, i * width : (i + 1) * width]
            order = ends[::-1] if len(flows) in FAR_FIRST else ends
            flows.append(reduce_all(*refs, *order, col))
        advance(("start", t))

    mine = pl.multiple_of(base + low * piece, 8)
    total = g_own[pl.ds(mine, piece), :]
    for d in range(1, inner):
        sent[-d].wait()
        total = total + g_in[d - 1]
    g_mid[high] = total
    sent = []
    for d in range(1, outer_):
        sent.append(send(g_mid.at[high], g_mid.at[high], g_sem, used, far(d), col))
        used += 1
    advance("gram sent")
    for copy in sent:
        copy.wait()
    total = g_mid[0]
    for q in range(1, outer_):
        total = total + g_mid[q]
    g_all[pl.ds(mine, piece), :] = total
    sent = []
    for d in reversed(range(inner)):
        for e in all_cols:
            if d or e:
                at = g_all.at[pl.ds(mine, piece)]
                sent.append(send(at, at, g_sem, used, near(d), (col + e) % cols))
                used += 1
    advance("gram back")
    advance("gram last")
    for copy in sent:
        copy.wait()

    m_ref[:h, :h] = g_all[:h, :]
    m_ref[:h, h:] = g_all[h : 2 * h, :]
    m_ref[h:, h:] = g_all[2 * h :, :]
    m_ref[h:, :h] = jnp.zeros((h, h), f32)
    for b in range(m_ref.shape[0] // BLOCK):
        eliminate(m_ref, r_ref, w_ref, b)
        advance(b)
    share = part.shape[1]
    if sliced:
        part[...] = r_ref[:, pl.ds(pl.multiple_of(col * share, TILE), share)]
    else:
        part[...] = r_ref[...]

    w = w_ref[...]
    both = stacked(w, 1), stacked(product(stacked(w.T, 1), stacked(w, 0)), 1)
    for t in range(halves):
        at = slice(t * half, (t + 1) * half)
        for flow in flows[t * each : (t + 1) * each]:
            for _ in flow:
                pass
        cross = jnp.concatenate([cross_refs[6 * i + 4][...] for i in range(t * each, (t + 1) * each)], axis=1)
        right = stacked(cross, 0)
        x, z = (product(left, right) for left in both)
        coupling[:, at] = x
        update[:, at] = z.astype(jnp.bfloat16)


def solve(panel, slab, rows, cols):
    m, k = panel.shape
    width = slab.shape[1]
    inner, outer_ = levels(rows)
    h = k // 2
    split = cols if (3 * h) % (8 * inner * cols) == 0 else 1
    piece = 3 * h // split // inner
    sliced = (k // cols) % TILE == 0
    share = k // cols if sliced else k
    f32, bf16 = jnp.float32, jnp.bfloat16
    halves = 2 if width % (4 * TILE) == 0 else 1
    count = 4 if halves == 2 and k % (8 * rows) == 0 else halves
    g_copies = (inner - 1) + (outer_ - 1) + inner * (cols if split > 1 else 1) - 1
    hbm = pl.BlockSpec(memory_space=pl.ANY)
    scratch = [
        pltpu.VMEM((3 * h, h), f32),
        pltpu.VMEM((max(inner - 1, 1), piece, h), f32),
        pltpu.VMEM((outer_, piece, h), f32),
        pltpu.VMEM((3 * h, h), f32),
        pltpu.VMEM((k, k), f32),
        pltpu.VMEM((k, k), f32),
        pltpu.VMEM((k, k), f32),
        pltpu.SemaphoreType.DMA((PANEL_STEPS,)),
        pltpu.SemaphoreType.DMA((halves,)),
        pltpu.SemaphoreType.DMA((2, g_copies)),
    ]
    for i in range(count):
        scratch += reduce_scratch(k, width // count, *((outer_, inner) if i in FAR_FIRST else (inner, outer_)))
    part, coupling, update, panel, slab = pl.pallas_call(
        functools.partial(solve_kernel, inner, outer_, cols, split, 1.0 / (m * rows), halves, count, sliced),
        out_shape=(
            jax.ShapeDtypeStruct((k, share), f32),
            jax.ShapeDtypeStruct((k, width), f32),
            jax.ShapeDtypeStruct((k, width), bf16),
            jax.ShapeDtypeStruct((m, k), bf16),
            jax.ShapeDtypeStruct((m, width), bf16),
        ),
        in_specs=[hbm, hbm],
        out_specs=[pl.BlockSpec(memory_space=pltpu.VMEM)] * 5,
        scratch_shapes=scratch,
        compiler_params=pltpu.CompilerParams(collective_id=0, has_side_effects=True, vmem_limit_bytes=20 << 20),
        cost_estimate=pl.CostEstimate(flops=2 * m * k * (k + width), bytes_accessed=2 * m * (k + width), transcendentals=0),
        name="solve",
    )(panel, slab)
    if not sliced:
        part = lax.dynamic_slice_in_dim(part, lax.axis_index("col") * (k // cols), k // cols, 1)
    return part, coupling, update, panel, slab


def finish_kernel(chunks, part, coupling, update, panel, slab, part_out, coupling_out, out, kept, sems):
    copies = [
        pltpu.make_async_copy(coupling, coupling_out, sems.at[0]),
        pltpu.make_async_copy(part, part_out, sems.at[1]),
    ]
    for copy in copies:
        copy.start()
    rows = panel.shape[0] // chunks
    z = update[...]
    for t in range(chunks):
        at = pl.ds(t * rows, rows)
        taken = jnp.dot(panel[at, :], z, preferred_element_type=jnp.float32)
        kept[at, :] = (slab[at, :].astype(jnp.float32) - taken).astype(jnp.bfloat16)
        copies.append(pltpu.make_async_copy(kept.at[at], out.at[at], sems.at[2 + t]))
        copies[-1].start()
    for copy in copies:
        copy.wait()


def finish(part, coupling, update, panel, slab):
    m, k = panel.shape
    width = slab.shape[1]
    chunks = 16
    return pl.pallas_call(
        functools.partial(finish_kernel, chunks),
        out_shape=(
            jax.ShapeDtypeStruct(part.shape, part.dtype),
            jax.ShapeDtypeStruct(coupling.shape, coupling.dtype),
            jax.ShapeDtypeStruct((m, width), jnp.bfloat16),
        ),
        in_specs=[pl.BlockSpec(memory_space=pltpu.VMEM)] * 5,
        out_specs=[pl.BlockSpec(memory_space=pl.ANY)] * 3,
        scratch_shapes=[pltpu.VMEM((m, width), jnp.bfloat16), pltpu.SemaphoreType.DMA((2 + chunks,))],
        compiler_params=pltpu.CompilerParams(vmem_limit_bytes=12 << 20),
        cost_estimate=pl.CostEstimate(flops=2 * m * k * width, bytes_accessed=2 * m * (k + 2 * width), transcendentals=0),
        name="finish",
    )(part, coupling, update, panel, slab)


def on_device(panel, slab):
    rows, cols = lax.axis_size("row"), lax.axis_size("col")
    there = [pltpu.with_memory_space_constraint(x, pltpu.HBM) for x in (panel, slab)]
    part, coupling, update, panel, slab = solve(*there, rows, cols)
    return finish(part, coupling, update, panel, slab)


def solution(mesh):
    from jax.sharding import PartitionSpec as P

    return jax.shard_map(
        on_device,
        mesh=mesh,
        in_specs=(P("row", None), P("row", "col")),
        out_specs=(P(None, "col"), P(None, "col"), P("row", "col")),
        check_vma=False,
    )
```
